32 devices in a mesh: dp: 8 (over z, x), shard: 4 (over y, core).
Axes of the slice: x: 2, y: 2, z: 4, core: 2. Of those that a mesh axis runs over, the one named last changes fastest.
Arguments:
- tokens: float32 [32, 4, 512, 384], P(('dp', 'shard')), may hold values from -40 to 40
- out_grad: float32 [32, 4, 512, 384], P(('dp', 'shard')), may hold values from -6 to 6
- cls_grad: float32 [1792, 384], P(('dp', 'shard')), may hold values from -6 to 6
- crop_lengths: int32 [32, 4, 13], P(('dp', 'shard')), may hold values from 0 to 197, as said below
- cls_route: int32 [32, 4, 13], P(('dp', 'shard')), may hold values from -1 to 55, as said below
- weight_qkv: float32 [442368], P(('dp', 'shard')), may hold values from -0.3125 to 0.3125
- weight_out: float32 [147456], P(('dp', 'shard')), may hold values from -0.75 to 0.75
- weight_up: float32 [589824], P(('dp', 'shard')), may hold values from -0.3125 to 0.3125
- weight_down: float32 [589824], P(('dp', 'shard')), may hold values from -0.15625 to 0.15625
- vectors: float32 [4608], P(('dp', 'shard')), may hold values from -0.9 to 3.5
- first_qkv: float32 [442368], P(('dp', 'shard')), may hold values from -0.00048828125 to 0.00048828125
- first_out: float32 [147456], P(('dp', 'shard')), may hold values from -0.00048828125 to 0.00048828125
- first_up: float32 [589824], P(('dp', 'shard')), may hold values from -0.00048828125 to 0.00048828125
- first_down: float32 [589824], P(('dp', 'shard')), may hold values from -0.00048828125 to 0.00048828125
- first_vectors: float32 [4608], P(('dp', 'shard')), may hold values from -0.001953125 to 0.001953125
- second_qkv: float32 [442368], P(('dp', 'shard')), may hold values from 2.8183622e-10 to 4.5093795e-09
- second_out: float32 [147456], P(('dp', 'shard')), may hold values from 2.8183622e-10 to 4.5093795e-09
- second_up: float32 [589824], P(('dp', 'shard')), may hold values from 2.8183622e-10 to 4.5093795e-09
- second_down: float32 [589824], P(('dp', 'shard')), may hold values from 2.8183622e-10 to 4.5093795e-09
- second_vectors: float32 [4608], P(('dp', 'shard')), may hold values from 4.5093795e-09 to 7.215007e-08
Outputs:
- block_out: float32 [32, 4, 512, 384], P(('dp', 'shard'))
- cls_grouped: float32 [1792, 384], P(('dp', 'shard'))
- input_grad: float32 [32, 4, 512, 384], P(('dp', 'shard'))
- grad_norm: float32 [], replicated
- updated_qkv: float32 [442368], P(('dp', 'shard'))
- updated_out: float32 [147456], P(('dp', 'shard'))
- updated_up: float32 [589824], P(('dp', 'shard'))
- updated_down: float32 [589824], P(('dp', 'shard'))
- updated_vectors: float32 [4608], P(('dp', 'shard'))
- mean_qkv: float32 [442368], P(('dp', 'shard'))
- mean_out: float32 [147456], P(('dp', 'shard'))
- mean_up: float32 [589824], P(('dp', 'shard'))
- mean_down: float32 [589824], P(('dp', 'shard'))
- mean_vectors: float32 [4608], P(('dp', 'shard'))
- square_qkv: float32 [442368], P(('dp', 'shard'))
- square_out: float32 [147456], P(('dp', 'shard'))
- square_up: float32 [589824], P(('dp', 'shard'))
- square_down: float32 [589824], P(('dp', 'shard'))
- square_vectors: float32 [4608], P(('dp', 'shard'))
The draws below stay inside these ranges and needn't reach their ends.
Inputs may be any that keep to these rules, and one draw needn't show every extreme that they name: `crop_lengths`: devices of even dp index hold 2 global views of 197 tokens in their first slots; the others hold focal crops of 37 tokens in their first slots, a number that varies by device and micro-batch; later slots are 0. `cls_route`: A slot is routed exactly when its length is not 0; values of one device are distinct and name owner group r // 7 of the same shard index and slot r % 7; at most 7 rows of one device go to one owner, and some owner receives 7 rows from every device of its shard index.
All inputs are finite; a program needn't handle non-finite values.
Results may differ from the reference program's by a relative error of at most 0.012.
The reference program's roundings to bfloat16 on the way count: a program that leaves them out, or rounds other values in their place, can miss the bound.
Values may be sent and summed in bfloat16 or wider, within the bound.
A program may use at most 192 MiB of HBM per device.

```python
import math
import jax
import jax.numpy as jnp
from jax import lax

D = 384
H = 6
HD = 64
FF = 1536
LG = 197
LF = 37
GV_DEV = 2
SLOTS = 13
TOK_DEV = 512
MICRO = 4
STEP_NUM = 10
GROUPS = 8
MEMBERS = 4
CAP = 7
PARAMS = 1774080


def crop_layout(key):
    devices = GROUPS * MEMBERS
    keys_all = jax.random.split(jax.random.fold_in(key, 11), 4)
    device_ids = jnp.arange(devices, dtype=jnp.int32)
    is_global = device_ids // MEMBERS % 2 == 0
    live_focal = jax.random.randint(keys_all[0], (devices, MICRO), SLOTS // 3, SLOTS + 1)
    chosen = jax.random.randint(keys_all[1], (MICRO,), 0, devices // 2)
    focal_device = (2 * (chosen // MEMBERS) + 1) * MEMBERS + chosen % MEMBERS
    live_focal = jnp.where(device_ids[:, None] == focal_device[None, :], SLOTS, live_focal)
    slot_ids = jnp.arange(SLOTS, dtype=jnp.int32)
    global_lengths = jnp.where(slot_ids < GV_DEV, LG, 0)
    focal_lengths = jnp.where(slot_ids[None, None, :] < live_focal[:, :, None], LF, 0)
    lengths = jnp.where(is_global[:, None, None], global_lengths[None, None, :], focal_lengths).astype(jnp.int32)
    live_slots = (lengths > 0).reshape(devices, MICRO * SLOTS)
    live_rank = jnp.cumsum(live_slots.astype(jnp.int32), axis=1) - 1
    anchor = GROUPS - 1
    random_keys = jax.random.randint(keys_all[3], (devices, GROUPS), 0, 1 << 20)
    group_ids = jnp.arange(GROUPS, dtype=jnp.int32)
    ordering = random_keys * GROUPS + group_ids[None, :]
    ordering = jnp.where(group_ids[None, :] == anchor, -1, ordering)
    owner_order = jnp.argsort(ordering, axis=1, stable=True).astype(jnp.int32)
    owner_group = jnp.take_along_axis(owner_order, jnp.clip(live_rank // CAP, 0, GROUPS - 1), axis=1)
    routes = jnp.where(live_slots, owner_group * CAP + live_rank % CAP, -1)
    return (lengths, routes.reshape(devices, MICRO, SLOTS).astype(jnp.int32))


def draw_crop_lengths(key, part):
    return crop_layout(key)[0]


def draw_cls_route(key, part):
    return crop_layout(key)[1]


def draw_tokens(key, part):
    keys_all = jax.random.split(jax.random.fold_in(key, 3), 3)
    devices = GROUPS * MEMBERS
    shape_all = (devices, MICRO, TOK_DEV, D)
    row_scale = jnp.exp(jax.random.uniform(keys_all[0], (devices, MICRO, TOK_DEV, 1), minval=math.log(0.5), maxval=math.log(2.5)))
    column_scale = jnp.exp(jax.random.uniform(keys_all[1], (D,), minval=math.log(0.4), maxval=math.log(4.0)))
    base = jnp.clip(jax.random.normal(keys_all[2], shape_all), -4.0, 4.0)
    return (base * row_scale * column_scale).astype(jnp.float32)


def draw_vectors(key, part):
    keys_all = jax.random.split(jax.random.fold_in(key, 5), 2)
    devices = GROUPS * MEMBERS
    device_of_row = jnp.arange(D) * devices // D
    along_groups = (device_of_row // MEMBERS).astype(jnp.float32) / max(GROUPS - 1, 1)
    along_members = (device_of_row % MEMBERS).astype(jnp.float32) / max(MEMBERS - 1, 1)
    rise = 3.0
    biases = 0.3 * jnp.clip(jax.random.normal(keys_all[0], (6 * D + FF,)), -3.0, 3.0)
    ramp = 0.6 * rise ** (0.5 * (along_groups + along_members))
    gains = ramp[None, :] * jax.random.uniform(keys_all[1], (2, D), minval=0.85, maxval=1.15)
    joined = jnp.concatenate([gains[0], biases[0:D], biases[D:2 * D], biases[2 * D:3 * D], biases[3 * D:4 * D], gains[1], biases[4 * D:5 * D], biases[5 * D:]])
    return joined.astype(jnp.float32)


def level_of(key, extent, cuts, least, high):
    def one(dim, shards_of):
        draws = jax.random.uniform(jax.random.fold_in(jax.random.fold_in(key, 6), dim), (shards_of,), jnp.float32, least / len(cuts), high / len(cuts))
        return jnp.repeat(jnp.exp(draws), extent[dim] // shards_of).reshape((-1,) + (1,) * (len(extent) - dim - 1))

    level = one(*cuts[0])
    for cut in cuts[1:]:
        level = level * one(*cut)
    return level


def bell_draw(stream_key, extent, scale, most, shards=(), kind=jnp.bfloat16):
    drawn = scale * jax.random.normal(stream_key, extent, jnp.float32)
    if shards:
        drawn = drawn * level_of(stream_key, extent, shards, -0.22, 0.18)
    return jnp.clip(drawn, -most, most).astype(kind)


def setup_inputs(seed: int = 0) -> dict:
    keys = jax.random.split(jax.random.key(seed), 21)
    return {
        "tokens": draw_tokens(jax.random.fold_in(keys[20], 71), 0),
        "out_grad": bell_draw(keys[1], (GROUPS * MEMBERS, MICRO, TOK_DEV, D), 1.0, 6.0, ((0, 32),), jnp.float32),
        "cls_grad": bell_draw(keys[2], (GROUPS * MEMBERS * GROUPS * CAP, D), 1.0, 6.0, ((0, 32),), jnp.float32),
        "crop_lengths": draw_crop_lengths(jax.random.fold_in(keys[20], 71), 0),
        "cls_route": draw_cls_route(jax.random.fold_in(keys[20], 71), 0),
        "weight_qkv": bell_draw(keys[5], (3 * D * D,), D ** -0.5, 0.3125, ((0, 32),), jnp.float32),
        "weight_out": bell_draw(keys[6], (D * D,), (D * LF // LG) ** -0.5, 0.75, ((0, 32),), jnp.float32),
        "weight_up": bell_draw(keys[7], (D * FF,), D ** -0.5, 0.3125, ((0, 32),), jnp.float32),
        "weight_down": bell_draw(keys[8], (FF * D,), FF ** -0.5, 0.15625, ((0, 32),), jnp.float32),
        "vectors": draw_vectors(jax.random.fold_in(keys[20], 71), 0),
        "first_qkv": bell_draw(keys[10], (3 * D * D,), (0.111 / PARAMS ** 0.5), 0.00048828125, ((0, 32),), jnp.float32),
        "first_out": bell_draw(keys[11], (D * D,), (0.111 / PARAMS ** 0.5), 0.00048828125, ((0, 32),), jnp.float32),
        "first_up": bell_draw(keys[12], (D * FF,), (0.111 / PARAMS ** 0.5), 0.00048828125, ((0, 32),), jnp.float32),
        "first_down": bell_draw(keys[13], (FF * D,), (0.111 / PARAMS ** 0.5), 0.00048828125, ((0, 32),), jnp.float32),
        "first_vectors": bell_draw(keys[14], (8 * D + FF,), (0.444 / PARAMS ** 0.5), 0.001953125, ((0, 32),), jnp.float32),
        "second_qkv": jnp.clip(jnp.exp(math.log(4.509379536443703e-09) - 2.7725887 * jax.random.uniform(keys[15], (3 * D * D,), jnp.float32) ** level_of(keys[15], (3 * D * D,), ((0, 32),), -0.2, 0.2)), 2.8183622102773143e-10, 4.509379536443703e-09),
        "second_out": jnp.clip(jnp.exp(math.log(4.509379536443703e-09) - 2.7725887 * jax.random.uniform(keys[16], (D * D,), jnp.float32) ** level_of(keys[16], (D * D,), ((0, 32),), -0.2, 0.2)), 2.8183622102773143e-10, 4.509379536443703e-09),
        "second_up": jnp.clip(jnp.exp(math.log(4.509379536443703e-09) - 2.7725887 * jax.random.uniform(keys[17], (D * FF,), jnp.float32) ** level_of(keys[17], (D * FF,), ((0, 32),), -0.2, 0.2)), 2.8183622102773143e-10, 4.509379536443703e-09),
        "second_down": jnp.clip(jnp.exp(math.log(4.509379536443703e-09) - 2.7725887 * jax.random.uniform(keys[18], (FF * D,), jnp.float32) ** level_of(keys[18], (FF * D,), ((0, 32),), -0.2, 0.2)), 2.8183622102773143e-10, 4.509379536443703e-09),
        "second_vectors": jnp.clip(jnp.exp(math.log(7.215007258309925e-08) - 2.7725887 * jax.random.uniform(keys[19], (8 * D + FF,), jnp.float32) ** level_of(keys[19], (8 * D + FF,), ((0, 32),), -0.2, 0.2)), 4.509379536443703e-09, 7.215007258309925e-08),
    }


NORM_EPSILON = 1e-06
BETA_ONE = 0.9
BETA_TWO = 0.999
ADAM_EPSILON = 1e-08
RATE_MATRIX = 0.05
RATE_VECTOR = 0.3
WEIGHT_DECAY = 0.05
CLIP_LIMIT = 1.0
MASK_VALUE = -1e+30
PRECISE = lax.Precision.HIGHEST

@jax.custom_vjp
def low(v):
    return lax.optimization_barrier(v.astype(jnp.bfloat16)).astype(jnp.float32)

@jax.custom_vjp
def low_back(v):
    return v

def low_keep(v):
    return (low(v), None)

def low_pass(kept, grad):
    return (grad,)

def back_keep(v):
    return (v, None)

def back_low(kept, grad):
    return (low(grad),)
low.defvjp(low_keep, low_pass)
low_back.defvjp(back_keep, back_low)

def layer_norm(inputs, gain_vec, offset_vec):
    average = lax.optimization_barrier(jnp.mean(inputs, axis=-1, keepdims=True))
    centred = inputs - average
    variance = lax.optimization_barrier(jnp.mean(centred * centred, axis=-1, keepdims=True))
    return centred * lax.rsqrt(variance + NORM_EPSILON) * gain_vec + offset_vec

def matmul(left, right):
    return jnp.dot(left, right, precision=PRECISE, preferred_element_type=jnp.float32)

def crop_segments(lengths, token_count):
    finish = jnp.cumsum(lengths).astype(jnp.int32)
    starts = (finish - lengths).astype(jnp.int32)
    places = jnp.arange(token_count, dtype=jnp.int32)
    segment = lax.optimization_barrier(jnp.sum((places[:, None] >= finish[None, :]).astype(jnp.int32), axis=1)).astype(jnp.int32)
    live_rows = places < finish[-1]
    return (segment, live_rows, starts)

def unpack(lowered):
    full_qkv, full_out, full_up, full_down, vector_all = lowered
    pieces = [vector_all[position * D:(position + 1) * D] for position in range(8)]
    pieces.append(vector_all[8 * D:])
    return (full_qkv.reshape(D, 3 * D), full_out.reshape(D, D), full_up.reshape(D, FF), full_down.reshape(FF, D), pieces)

def buffer_forward(full, inputs, segment, live_rows):
    full_qkv, full_out, full_up, full_down, pieces = full
    gain_one, offset_one, bias_query, bias_value, bias_out, gain_two, offset_two, bias_down, bias_up = pieces
    count = inputs.shape[0]
    normed_one = low(layer_norm(inputs, gain_one, offset_one))
    proj_bias = jnp.concatenate([bias_query, jnp.zeros((D,), jnp.float32), bias_value])
    projected = low(low_back(matmul(normed_one, full_qkv) + proj_bias))
    queries = projected[:, :D].reshape(count, H, HD)
    key_rows = projected[:, D:2 * D].reshape(count, H, HD)
    values = projected[:, 2 * D:].reshape(count, H, HD)
    raw = jnp.einsum('qhe,khe->hqk', queries, key_rows, precision=PRECISE) * HD ** (-0.5)
    raw = low_back(raw)
    allowed = segment[:, None] == segment[None, :]
    scores = jnp.where(allowed[None], raw, MASK_VALUE)
    row_max = lax.optimization_barrier(jnp.max(scores, axis=-1, keepdims=True))
    exponent = jnp.exp(scores - row_max)
    probability = low(exponent / lax.optimization_barrier(jnp.sum(exponent, axis=-1, keepdims=True)))
    attended = jnp.einsum('hqk,khe->qhe', probability, values, precision=PRECISE).reshape(count, D)
    attended = low(low_back(attended))
    branch = low_back(matmul(attended, full_out) + bias_out)
    middle = inputs + branch
    normed_two = low(layer_norm(middle, gain_two, offset_two))
    hidden_pre = low_back(matmul(normed_two, full_up) + bias_up)
    activated = low(jax.nn.gelu(hidden_pre, approximate=False))
    down_part = low_back(matmul(activated, full_down) + bias_down)
    return jnp.where(live_rows[:, None], middle + down_part, 0.0)

def adam_update(master, moment_one, second, gradient, factor, step_rate, decay_rate):
    clipped = gradient * factor
    mean_new = BETA_ONE * moment_one + (1.0 - BETA_ONE) * clipped
    square_new = BETA_TWO * second + (1.0 - BETA_TWO) * clipped * clipped
    mean_hat = mean_new / (1.0 - BETA_ONE ** STEP_NUM)
    square_hat = square_new / (1.0 - BETA_TWO ** STEP_NUM)
    updated = master - step_rate * (mean_hat / (jnp.sqrt(square_hat) + ADAM_EPSILON) + decay_rate * master)
    return (updated, mean_new, square_new)

def reference(tokens, out_grad, cls_grad, crop_lengths, cls_route, weight_qkv, weight_out, weight_up, weight_down, vectors, first_qkv, first_out, first_up, first_down, first_vectors, second_qkv, second_out, second_up, second_down, second_vectors):
    devices = GROUPS * MEMBERS
    buffers = devices * MICRO
    flat_lengths = crop_lengths.reshape(buffers, SLOTS)
    segment, live_rows, starts = jax.vmap(lambda lengths: crop_segments(lengths, TOK_DEV))(flat_lengths)
    routes = cls_route.reshape(devices, MICRO * SLOTS)
    device_ids = jnp.arange(devices, dtype=jnp.int32)[:, None]
    source_group = device_ids // MEMBERS
    member = device_ids % MEMBERS
    target = (routes // CAP * MEMBERS + member) * (GROUPS * CAP) + source_group * CAP + routes % CAP
    target = jnp.where(routes >= 0, target, devices * GROUPS * CAP).astype(jnp.int32)

    def forward(params, inputs_all):
        full = unpack(tuple((low(master) for master in params)))
        block = jax.checkpoint(buffer_forward)
        results = lax.map(lambda operands: block(full, operands[0], operands[1], operands[2]), (inputs_all.reshape(buffers, TOK_DEV, D), segment, live_rows))
        block_out = results.reshape(devices, MICRO, TOK_DEV, D)
        picked = jax.vmap(lambda rows_all, places: rows_all[places])(results, jnp.clip(starts, 0, TOK_DEV - 1))
        picked = picked.reshape(devices * MICRO * SLOTS, D)
        cls_grouped = jnp.zeros((devices * GROUPS * CAP, D), jnp.float32).at[target.reshape(-1)].add(picked, mode='drop')
        return (block_out, cls_grouped)
    params = (weight_qkv, weight_out, weight_up, weight_down, vectors)
    (block_out, cls_grouped), pullback = jax.vjp(forward, params, tokens)
    grad_params, input_grad = pullback((out_grad, cls_grad))
    total = jnp.float32(0.0)
    for gradient in grad_params:
        total = total + jnp.sum(gradient * gradient)
    grad_norm = jnp.sqrt(total)
    factor = jnp.minimum(1.0, CLIP_LIMIT / grad_norm)
    firsts = (first_qkv, first_out, first_up, first_down, first_vectors)
    seconds = (second_qkv, second_out, second_up, second_down, second_vectors)
    rates = (RATE_MATRIX, RATE_MATRIX, RATE_MATRIX, RATE_MATRIX, RATE_VECTOR)
    decays = (WEIGHT_DECAY, WEIGHT_DECAY, WEIGHT_DECAY, WEIGHT_DECAY, 0.0)
    results_new = [adam_update(params[position], firsts[position], seconds[position], grad_params[position], factor, rates[position], decays[position]) for position in range(5)]
    updated = [entry[0] for entry in results_new]
    means = [entry[1] for entry in results_new]
    squares = [entry[2] for entry in results_new]
    return (block_out, cls_grouped, input_grad, grad_norm, updated[0], updated[1], updated[2], updated[3], updated[4], means[0], means[1], means[2], means[3], means[4], squares[0], squares[1], squares[2], squares[3], squares[4])
```

```python
import functools

import jax
import jax.numpy as jnp
from jax import lax
from jax.experimental import pallas as pl
from jax.experimental.pallas import tpu as pltpu
from jax.sharding import PartitionSpec as P

D = 384
H = 6
HD = 64
FF = 1536
STEP_NUM = 10
LG = 197
LF = 37

NORM_EPSILON = 1e-06
BETA_ONE = 0.9
BETA_TWO = 0.999
ADAM_EPSILON = 1e-08
RATE_MATRIX = 0.05
RATE_VECTOR = 0.3
WEIGHT_DECAY = 0.05
CLIP_LIMIT = 1.0
MASK_VALUE = -1e30

BF = jnp.bfloat16
F32 = jnp.float32
NN = (((1,), (0,)), ((), ()))
NT = (((1,), (1,)), ((), ()))
TN = (((0,), (0,)), ((), ()))
PAIRS = H // 2
CHUNKS = FF // D
TILE = 128
WIN = 256


def dg(a, b, dims):
    return lax.dot_general(a, b, dims, preferred_element_type=F32)


def iota(shape, dim):
    return lax.broadcasted_iota(jnp.int32, shape, dim)


def tiles(is_global):
    focal = ((0, 0, 0, 128), (128, 64, 128, 256), (256, 192, 256, 384), (384, 256, 384, 512))
    whole = ((0, 0, 0, 128), (80, 0, 128, 197), (192, 192, 197, 320), (272, 192, 320, 394))
    return [
        tuple(jnp.where(is_global, w, f) for w, f in zip(whole[i], focal[i])) for i in range(4)
    ]


def norm_stats(v):
    mean = jnp.mean(v, axis=-1, keepdims=True)
    c = v - mean
    var = jnp.mean(c * c, axis=-1, keepdims=True)
    r = lax.rsqrt(var + NORM_EPSILON)
    return c * r, r


def norm_back(dh, gain, xhat, r):
    d = dh * gain
    m1 = jnp.mean(d, axis=-1, keepdims=True)
    m2 = jnp.mean(d * xhat, axis=-1, keepdims=True)
    return (d - m1 - xhat * m2) * r


def gelu_parts(u):
    cdf = 0.5 + 0.5 * lax.erf(u * 0.7071067811865476)
    pdf = jnp.exp(u * u * -0.5) * 0.3989422804014327
    return u * cdf, cdf + u * pdf


def main_kernel(
    lengths, routes, x_hbm, og_hbm, wa, wu, wd, vec, ret,
    out_hbm, ig_hbm, ga, gu, gd, gvec, heads,
    x, dy, y, m, dh, h1, h1t, p, att, o, h2, h2t, dy16, dy16t, dp, gdt, bias, sem,
    *, capacity, owners, stages
):
    batches, rows = x.shape[0], x.shape[1]
    slots = lengths.shape[1]
    cap_pad = ret.shape[0] // owners
    is_global = lax.axis_index("dp") % 2 == 0
    length = jnp.where(is_global, LG, LF)
    layout = tiles(is_global)

    copies = [
        pltpu.make_async_copy(x_hbm.at[0, b], x.at[b], sem.at[b]) for b in range(batches)
    ] + [
        pltpu.make_async_copy(og_hbm.at[0, b], dy.at[b], sem.at[batches + b])
        for b in range(batches)
    ]
    for c in copies:
        c.start()

    def segment_of(t):
        return jnp.where(
            is_global,
            (t >= LG).astype(jnp.int32) + (t >= 2 * LG).astype(jnp.int32),
            lax.shift_right_logical(t * 1772, 16),
        )

    for i, (q0, k0, lo, hi) in enumerate(layout):
        keys = segment_of(iota((WIN, TILE), 0) + k0)
        queries = segment_of(iota((WIN, TILE), 1) + q0)
        mask = jnp.where(keys == queries, 0.0, MASK_VALUE).astype(F32)
        bias[i, :, :TILE] = mask
        bias[i, :, TILE:] = mask

    def v(row):
        return vec[row : row + 1, :]

    low_half = iota((TILE, TILE), 1) < HD

    def stack(t):
        z = jnp.zeros_like(t)
        return jnp.concatenate([jnp.where(low_half, t, z), jnp.where(low_half, z, t)], axis=0)

    def unstack(t):
        return jnp.where(low_half, t[:TILE], t[TILE:])

    def rows_at(b):
        return pl.ds(pl.multiple_of(b * rows, rows), rows)

    gvec[...] = jnp.zeros_like(gvec)
    if "f1" in stages:
        for b in range(batches):
            copies[b].wait()

        def attend(b, c):
            rs = rows_at(b)
            xhat, _ = norm_stats(x[b])
            h = (xhat * v(0) + v(1)).astype(BF)
            h1[rs, :] = h
            h1t[:, rs] = h.T
            p[rs, 0:D] = (dg(h, wa[:, 0:D], NN) + v(2)).astype(BF)
            p[rs, D : 2 * D] = dg(h, wa[:, D : 2 * D], NN).astype(BF)
            p[rs, 2 * D : 3 * D] = (dg(h, wa[:, 2 * D : 3 * D], NN) + v(3)).astype(BF)
            for pair in range(PAIRS if "at" in stages else 0):
                c0 = pair * TILE
                for i, (q0, k0, lo, hi) in enumerate(layout):
                    qr = pl.ds(pl.multiple_of(b * rows + q0, 16), TILE)
                    kr = pl.ds(pl.multiple_of(b * rows + k0, 16), WIN)
                    q = stack(p[qr, pl.ds(c0, TILE)] * BF(HD**-0.5))
                    k = p[kr, pl.ds(D + c0, TILE)]
                    val = p[kr, pl.ds(2 * D + c0, TILE)]
                    s = dg(k, q, NT) + bias[i]
                    e = jnp.exp(s - jnp.max(s, axis=0, keepdims=True))
                    a = (e * (1.0 / jnp.sum(e, axis=0, keepdims=True))).astype(BF)
                    att[b, pair, i] = a
                    r = unstack(dg(a, val, TN)).astype(BF)
                    own = iota((TILE, TILE), 0) + q0
                    own = (own >= lo) & (own < hi)
                    old = o[qr, pl.ds(c0, TILE)]
                    o[qr, pl.ds(c0, TILE)] = jnp.where(own, r, old)
            return c

        o[...] = jnp.zeros_like(o)
        lax.fori_loop(0, batches, attend, 0)

    def live_of(b):
        n = lengths[b, 0]
        for k in range(1, slots):
            n = n + lengths[b, k]
        return n

    def places(b, r):
        spot = jnp.full(r.shape, -1, jnp.int32)
        for k in range(slots):
            route = routes[b, k]
            padded = (route // capacity) * cap_pad + route % capacity
            padded = jnp.where(route >= 0, padded, -1)
            spot = jnp.where(r == padded, k * length, spot)
        return spot

    if "f1b" in stages:
        for b in range(batches):
            copies[batches + b].wait()

        def middle(b, c):
            rs = rows_at(b)
            mid = x[b] + (dg(o[rs, :], wa[:, 3 * D :], NN) + v(4))
            m[b] = mid
            xhat, _ = norm_stats(mid)
            h = (xhat * v(5) + v(6)).astype(BF)
            h2[rs, :] = h
            h2t[:, rs] = h.T
            nr = ret.shape[0]
            pick = (iota((rows, nr), 0) == places(b, iota((1, nr), 1))).astype(BF)
            live = iota((rows, D), 0) < live_of(b)
            g = dy[b] + dg(pick, ret[...].astype(BF), NN)
            g = jnp.where(live, g, 0.0)
            dy[b] = g
            g16 = g.astype(BF)
            dy16[rs, :] = g16
            dy16t[:, rs] = g16.T
            gvec[7:8, :] += jnp.sum(g16.astype(F32), axis=0, keepdims=True)
            y[b] = jnp.zeros((rows, D), F32)
            dh[b] = jnp.zeros((rows, D), F32)
            return c

        lax.fori_loop(0, batches, middle, 0)

    if "f2" in stages:
        gu[...] = jnp.zeros_like(gu)
        gdt[...] = jnp.zeros_like(gdt)

        def mlp(t, c):
            j, b = t // batches, t % batches
            rs = rows_at(b)
            cs = pl.ds(pl.multiple_of(j * D, D), D)
            u = dg(h2[rs, :], wu[:, cs], NN) + vec[pl.ds(8 + j, 1), :]
            g, slope = gelu_parts(u)
            g = g.astype(BF)
            y[b] += dg(g, wd[cs, :], NN)
            gdt[:, cs] += dg(dy16t[:, rs], g, NN)
            du = (dg(dy16[rs, :], wd[cs, :], NT) * slope).astype(BF)
            gu[:, cs] += dg(h2t[:, rs], du, NN)
            dh[b] += dg(du, wu[:, cs], NT)
            gvec[pl.ds(8 + j, 1), :] += jnp.sum(du.astype(F32), axis=0, keepdims=True)
            return c

        lax.fori_loop(0, CHUNKS * batches, mlp, 0)
        for j in range(CHUNKS):
            gd[j * D : (j + 1) * D, :] = gdt[:, j * D : (j + 1) * D].T

    if "f2b" in stages:
        ga[:, 3 * D :] = jnp.zeros((D, D), F32)
        heads[...] = jnp.zeros_like(heads)

        def turn(b, c):
            rs = rows_at(b)
            mid = m[b]
            live = iota((rows, D), 0) < live_of(b)
            out = jnp.where(live, mid + (y[b] + v(7)), 0.0)
            y[b] = out
            nr = heads.shape[0]
            pick = (places(b, iota((nr, 1), 0)) == iota((nr, rows), 1)).astype(BF)
            heads[...] += dg(pick, out.astype(BF), NN)
            xhat, r = norm_stats(mid)
            d2 = dh[b]
            gvec[5:6, :] += jnp.sum(d2 * xhat, axis=0, keepdims=True)
            gvec[6:7, :] += jnp.sum(d2, axis=0, keepdims=True)
            dm = dy[b] + norm_back(d2, v(5), xhat, r)
            dy[b] = dm
            d16 = dm.astype(BF)
            gvec[4:5, :] += jnp.sum(d16.astype(F32), axis=0, keepdims=True)
            ga[:, 3 * D :] += dg(o[rs, :], d16, TN)
            h2[rs, :] = dg(d16, wa[:, 3 * D :], NT).astype(BF)
            dh[b] = jnp.zeros((rows, D), F32)
            return c

        lax.fori_loop(0, batches, turn, 0)
        outs = [
            pltpu.make_async_copy(y.at[b], out_hbm.at[0, b], sem.at[b]) for b in range(batches)
        ]
        for c in outs:
            c.start()

    if "b1" in stages:
        for pair in range(PAIRS):
            c0 = pair * TILE

            def attend_back(b, c):
                rs = rows_at(b)
                y_k, y_v = m.at[0, :, 0:TILE], m.at[0, :, TILE : 2 * TILE]
                m[0, :, 0 : 2 * TILE] = jnp.zeros((rows, 2 * TILE), F32)
                for i, (q0, k0, lo, hi) in enumerate(layout):
                    qr = pl.ds(pl.multiple_of(b * rows + q0, 16), TILE)
                    kr = pl.ds(pl.multiple_of(b * rows + k0, 16), WIN)
                    wr = pl.ds(pl.multiple_of(k0, 16), WIN)
                    own = iota((TILE, TILE), 0) + q0
                    own = (own >= lo) & (own < hi)
                    do = h2[qr, pl.ds(c0, TILE)]
                    do = stack(jnp.where(own, do, jnp.zeros_like(do)))
                    q = stack(p[qr, pl.ds(c0, TILE)] * BF(HD**-0.5))
                    k = p[kr, pl.ds(D + c0, TILE)]
                    val = p[kr, pl.ds(2 * D + c0, TILE)]
                    a = att[b, pair, i]
                    af = a.astype(F32)
                    da = dg(val, do, NT)
                    ds = af * (da - jnp.sum(af * da, axis=0, keepdims=True))
                    ds = ds.astype(BF)
                    dq = (unstack(dg(ds, k, TN)) * HD**-0.5).astype(BF)
                    old = dp[qr, pl.ds(0, TILE)]
                    dp[qr, pl.ds(0, TILE)] = jnp.where(own, dq, old)
                    y_k[wr, :] += dg(ds, q, NN)
                    y_v[wr, :] += dg(a, do, NN)
                dp[rs, TILE : 2 * TILE] = y_k[...].astype(BF)
                dp[rs, 2 * TILE :] = y_v[...].astype(BF)
                w = jnp.concatenate(
                    [wa[:, s * D + c0 : s * D + c0 + TILE] for s in range(3)], axis=1
                )
                dh[b] += dg(dp[rs, :], w, NT)
                return c

            dp[:, 0:TILE] = jnp.zeros((batches * rows, TILE), BF)
            lax.fori_loop(0, batches, attend_back, 0)
            g = dg(h1t[...], dp[...], NN)
            sums = jnp.sum(dp[...].astype(F32), axis=0, keepdims=True)
            gvec[2:3, c0 : c0 + TILE] = sums[:, 0:TILE]
            gvec[3:4, c0 : c0 + TILE] = sums[:, 2 * TILE :]
            for s in range(3):
                ga[:, s * D + c0 : s * D + c0 + TILE] = g[:, s * TILE : (s + 1) * TILE]

    if "b2" in stages:
        for c in outs:
            c.wait()

        def last(b, c):
            xhat, r = norm_stats(x[b])
            d1 = dh[b]
            gvec[0:1, :] += jnp.sum(d1 * xhat, axis=0, keepdims=True)
            gvec[1:2, :] += jnp.sum(d1, axis=0, keepdims=True)
            y[b] = dy[b] + norm_back(d1, v(0), xhat, r)
            return c

        lax.fori_loop(0, batches, last, 0)
        outs = [
            pltpu.make_async_copy(y.at[b], ig_hbm.at[0, b], sem.at[b]) for b in range(batches)
        ]
        for c in outs:
            c.start()
        for c in outs:
            c.wait()


STAGES = ("f1", "at", "f1b", "f2", "f2b", "b1", "b2")


def run_main(lengths, routes, x, og, wa, wu, wd, vec, ret, capacity, owners, stages=STAGES):
    batches, rows = x.shape[1], x.shape[2]
    total = batches * rows
    vm = pl.BlockSpec(memory_space=pltpu.VMEM)
    sm = pl.BlockSpec(memory_space=pltpu.SMEM)
    anyspace = pl.BlockSpec(memory_space=pl.ANY)
    out_shape = (
        jax.ShapeDtypeStruct(x.shape, F32),
        jax.ShapeDtypeStruct(x.shape, F32),
        jax.ShapeDtypeStruct((D, 4 * D), F32),
        jax.ShapeDtypeStruct((D, FF), F32),
        jax.ShapeDtypeStruct((FF, D), F32),
        jax.ShapeDtypeStruct((16, D), F32),
        jax.ShapeDtypeStruct(ret.shape, F32),
    )
    act = pltpu.VMEM((total, D), BF)
    actt = pltpu.VMEM((D, total), BF)
    full = pltpu.VMEM((batches, rows, D), F32)
    scratch = [
        full, full, full, full, full,
        act, actt, pltpu.VMEM((total, 3 * D), BF),
        pltpu.VMEM((batches, PAIRS, 4, WIN, 2 * TILE), BF),
        act, act, actt, act, actt, act,
        pltpu.VMEM((D, FF), F32),
        pltpu.VMEM((4, WIN, 2 * TILE), F32),
        pltpu.SemaphoreType.DMA((2 * batches,)),
    ]
    return pl.pallas_call(
        functools.partial(main_kernel, capacity=capacity, owners=owners, stages=stages),
        out_shape=out_shape,
        in_specs=[sm, sm, anyspace, anyspace, vm, vm, vm, vm, vm],
        out_specs=(anyspace, anyspace, vm, vm, vm, vm, vm),
        scratch_shapes=scratch,
        compiler_params=pltpu.CompilerParams(vmem_limit_bytes=62 * 2**20),
        name="step_main",
    )(lengths, routes, x, og, wa, wu, wd, vec, ret)


def adam_update(master, moment_one, second, gradient, factor, step_rate, decay_rate):
    clipped = gradient * factor
    mean_new = BETA_ONE * moment_one + (1.0 - BETA_ONE) * clipped
    square_new = BETA_TWO * second + (1.0 - BETA_TWO) * clipped * clipped
    mean_hat = mean_new / (1.0 - BETA_ONE**STEP_NUM)
    square_hat = square_new / (1.0 - BETA_TWO**STEP_NUM)
    updated = master - step_rate * (
        mean_hat / (jnp.sqrt(square_hat) + ADAM_EPSILON) + decay_rate * master
    )
    return (updated, mean_new, square_new)


def pad_slots(a, owners, capacity, cap_pad):
    a = a.reshape(owners, capacity, D)
    return jnp.pad(a, ((0, 0), (0, cap_pad - capacity), (0, 0))).reshape(owners * cap_pad, D)


def local(tokens, out_grad, cls_grad, crop_lengths, cls_route, *state):
    masters, firsts, seconds = state[:5], state[5:10], state[10:15]
    axes = ("dp", "shard")
    owners = lax.axis_size("dp")
    capacity = cls_grad.shape[0] // owners
    cap_pad = -(-capacity // 8) * 8
    qkv, out, up, down, vector = (
        lax.all_gather(w.astype(BF), axes, axis=0, tiled=True) for w in masters
    )
    wa = jnp.concatenate([qkv.reshape(D, 3 * D), out.reshape(D, D)], axis=1)
    vec = jnp.pad(vector.astype(F32).reshape(12, D), ((0, 4), (0, 0)))
    returned = lax.all_to_all(
        cls_grad.reshape(owners, capacity, D).astype(BF), "dp", 0, 0, tiled=True
    )
    ret = pad_slots(returned.astype(F32), owners, capacity, cap_pad)
    block_out, input_grad, ga, gu, gd, gvec, heads = run_main(
        crop_lengths[0], cls_route[0], tokens, out_grad,
        wa, up.reshape(D, FF), down.reshape(FF, D), vec, ret, capacity, owners,
    )
    heads = heads.reshape(owners, cap_pad, D)[:, :capacity].astype(BF)
    cls_grouped = lax.all_to_all(heads, "dp", 0, 0, tiled=True).astype(F32)
    cls_grouped = cls_grouped.reshape(owners * capacity, D)
    grads = (ga[:, : 3 * D], ga[:, 3 * D :], gu, gd, gvec[:12])
    grads = [
        lax.psum_scatter(g.reshape(-1), axes, scatter_dimension=0, tiled=True) for g in grads
    ]
    grad_norm = jnp.sqrt(lax.psum(sum(jnp.sum(g * g) for g in grads), axes))
    factor = jnp.minimum(1.0, CLIP_LIMIT / grad_norm)
    rates = (RATE_MATRIX,) * 4 + (RATE_VECTOR,)
    decays = (WEIGHT_DECAY,) * 4 + (0.0,)
    new = [
        adam_update(masters[i], firsts[i], seconds[i], grads[i], factor, rates[i], decays[i])
        for i in range(5)
    ]
    return (block_out, cls_grouped, input_grad, grad_norm) + tuple(
        new[i][k] for k in range(3) for i in range(5)
    )


def solution(mesh):
    spread = ("dp", "shard")
    in_specs = (
        P(spread, None, None, None), P(spread, None, None, None), P(spread, None),
        P(spread, None, None), P(spread, None, None),
    ) + (P(spread),) * 15
    out_specs = (
        P(spread, None, None, None), P(spread, None), P(spread, None, None, None), P(),
    ) + (P(spread),) * 15
    return jax.shard_map(local, mesh=mesh, in_specs=in_specs, out_specs=out_specs, check_vma=False)
```

```python
import functools

import jax
import jax.numpy as jnp
from jax import lax
from jax.experimental import pallas as pl
from jax.experimental.pallas import tpu as pltpu
from jax.sharding import PartitionSpec as P

D = 384
H = 6
HD = 64
FF = 1536
STEP_NUM = 10
LG = 197
LF = 37

NORM_EPSILON = 1e-06
BETA_ONE = 0.9
BETA_TWO = 0.999
ADAM_EPSILON = 1e-08
RATE_MATRIX = 0.05
RATE_VECTOR = 0.3
WEIGHT_DECAY = 0.05
CLIP_LIMIT = 1.0
MASK_VALUE = -1e30

BF = jnp.bfloat16
F32 = jnp.float32
NN = (((1,), (0,)), ((), ()))
NT = (((1,), (1,)), ((), ()))
TN = (((0,), (0,)), ((), ()))
PAIRS = H // 2
CHUNKS = FF // D
TILE = 128
WIN = 256


def dg(a, b, dims):
    return lax.dot_general(a, b, dims, preferred_element_type=F32)


def iota(shape, dim):
    return lax.broadcasted_iota(jnp.int32, shape, dim)


def tiles(is_global):
    focal = ((0, 0, 0, 128), (128, 64, 128, 256), (256, 192, 256, 384), (384, 256, 384, 512))
    whole = ((0, 0, 0, 128), (80, 0, 128, 197), (192, 192, 197, 320), (272, 192, 320, 394))
    return [
        tuple(jnp.where(is_global, w, f) for w, f in zip(whole[i], focal[i])) for i in range(4)
    ]


def norm_stats(v):
    mean = jnp.mean(v, axis=-1, keepdims=True)
    c = v - mean
    var = jnp.mean(c * c, axis=-1, keepdims=True)
    r = lax.rsqrt(var + NORM_EPSILON)
    return c * r, r


def norm_back(dh, gain, xhat, r):
    d = dh * gain
    m1 = jnp.mean(d, axis=-1, keepdims=True)
    m2 = jnp.mean(d * xhat, axis=-1, keepdims=True)
    return (d - m1 - xhat * m2) * r


def gelu_parts(u):
    cdf = 0.5 + 0.5 * lax.erf(u * 0.7071067811865476)
    pdf = jnp.exp(u * u * -0.5) * 0.3989422804014327
    return u * cdf, cdf + u * pdf


def main_kernel(
    lengths, routes, x_hbm, og_hbm, wa, wu, wd, vec, ret,
    out_hbm, ig_hbm, ga, gu, gd, gvec, heads,
    x, dy, y, m, dh, h1, h1t, p, att, o, h2, h2t, dy16, dy16t, dp, gdt, bias, sem,
    *, capacity, owners, stages
):
    batches, rows = x.shape[0], x.shape[1]
    slots = lengths.shape[1]
    cap_pad = ret.shape[0] // owners
    is_global = lax.axis_index("dp") % 2 == 0
    length = jnp.where(is_global, LG, LF)
    layout = tiles(is_global)

    copies = [
        pltpu.make_async_copy(x_hbm.at[0, b], x.at[b], sem.at[b]) for b in range(batches)
    ] + [
        pltpu.make_async_copy(og_hbm.at[0, b], dy.at[b], sem.at[batches + b])
        for b in range(batches)
    ]
    for c in copies:
        c.start()

    def segment_of(t):
        return jnp.where(
            is_global,
            (t >= LG).astype(jnp.int32) + (t >= 2 * LG).astype(jnp.int32),
            lax.shift_right_logical(t * 1772, 16),
        )

    for i, (q0, k0, lo, hi) in enumerate(layout):
        keys = segment_of(iota((WIN, TILE), 0) + k0)
        queries = segment_of(iota((WIN, TILE), 1) + q0)
        mask = jnp.where(keys == queries, 0.0, MASK_VALUE).astype(F32)
        bias[i, :, :TILE] = mask
        bias[i, :, TILE:] = mask

    def v(row):
        return vec[row : row + 1, :]

    low_half = iota((TILE, TILE), 1) < HD

    def stack(t):
        z = jnp.zeros_like(t)
        return jnp.concatenate([jnp.where(low_half, t, z), jnp.where(low_half, z, t)], axis=0)

    def unstack(t):
        return jnp.where(low_half, t[:TILE], t[TILE:])

    def rows_at(b):
        return pl.ds(pl.multiple_of(b * rows, rows), rows)

    gvec[...] = jnp.zeros_like(gvec)
    if "f1" in stages:
        for b in range(batches):
            copies[b].wait()

        def attend(b, c):
            rs = rows_at(b)
            xhat, _ = norm_stats(x[b])
            h = (xhat * v(0) + v(1)).astype(BF)
            h1[rs, :] = h
            h1t[:, rs] = h.T
            p[rs, 0:D] = (dg(h, wa[:, 0:D], NN) + v(2)).astype(BF)
            p[rs, D : 2 * D] = dg(h, wa[:, D : 2 * D], NN).astype(BF)
            p[rs, 2 * D : 3 * D] = (dg(h, wa[:, 2 * D : 3 * D], NN) + v(3)).astype(BF)
            for pair in range(PAIRS if "at" in stages else 0):
                c0 = pair * TILE
                for i, (q0, k0, lo, hi) in enumerate(layout):
                    qr = pl.ds(pl.multiple_of(b * rows + q0, 16), TILE)
                    kr = pl.ds(pl.multiple_of(b * rows + k0, 16), WIN)
                    q = stack(p[qr, pl.ds(c0, TILE)] * BF(HD**-0.5))
                    k = p[kr, pl.ds(D + c0, TILE)]
                    val = p[kr, pl.ds(2 * D + c0, TILE)]
                    s = dg(k, q, NT) + bias[i]
                    e = jnp.exp(s - jnp.max(s, axis=0, keepdims=True))
                    a = (e * (1.0 / jnp.sum(e, axis=0, keepdims=True))).astype(BF)
                    att[b, pair, i] = a
                    r = unstack(dg(a, val, TN)).astype(BF)
                    own = iota((TILE, TILE), 0) + q0
                    own = (own >= lo) & (own < hi)
                    old = o[qr, pl.ds(c0, TILE)]
                    o[qr, pl.ds(c0, TILE)] = jnp.where(own, r, old)
            return c

        o[...] = jnp.zeros_like(o)
        lax.fori_loop(0, batches, attend, 0)

    def live_of(b):
        n = lengths[b, 0]
        for k in range(1, slots):
            n = n + lengths[b, k]
        return n

    def places(b, r):
        spot = jnp.full(r.shape, -1, jnp.int32)
        for k in range(slots):
            route = routes[b, k]
            padded = (route // capacity) * cap_pad + route % capacity
            padded = jnp.where(route >= 0, padded, -1)
            spot = jnp.where(r == padded, k * length, spot)
        return spot

    if "f1b" in stages:
        for b in range(batches):
            copies[batches + b].wait()

        def middle(b, c):
            rs = rows_at(b)
            mid = x[b] + (dg(o[rs, :], wa[:, 3 * D :], NN) + v(4))
            m[b] = mid
            xhat, _ = norm_stats(mid)
            h = (xhat * v(5) + v(6)).astype(BF)
            h2[rs, :] = h
            h2t[:, rs] = h.T
            nr = ret.shape[0]
            pick = (iota((rows, nr), 0) == places(b, iota((1, nr), 1))).astype(BF)
            live = iota((rows, D), 0) < live_of(b)
            g = dy[b] + dg(pick, ret[...].astype(BF), NN)
            g = jnp.where(live, g, 0.0)
            dy[b] = g
            g16 = g.astype(BF)
            dy16[rs, :] = g16
            dy16t[:, rs] = g16.T
            gvec[7:8, :] += jnp.sum(g16.astype(F32), axis=0, keepdims=True)
            y[b] = jnp.zeros((rows, D), F32)
            dh[b] = jnp.zeros((rows, D), F32)
            return c

        lax.fori_loop(0, batches, middle, 0)

    if "f2" in stages:
        gu[...] = jnp.zeros_like(gu)
        gdt[...] = jnp.zeros_like(gdt)

        def mlp(t, c):
            j, b = t // batches, t % batches
            rs = rows_at(b)
            cs = pl.ds(pl.multiple_of(j * D, D), D)
            u = dg(h2[rs, :], wu[:, cs], NN) + vec[pl.ds(8 + j, 1), :]
            g, slope = gelu_parts(u)
            g = g.astype(BF)
            y[b] += dg(g, wd[cs, :], NN)
            gdt[:, cs] += dg(dy16t[:, rs], g, NN)
            du = (dg(dy16[rs, :], wd[cs, :], NT) * slope).astype(BF)
            gu[:, cs] += dg(h2t[:, rs], du, NN)
            dh[b] += dg(du, wu[:, cs], NT)
            gvec[pl.ds(8 + j, 1), :] += jnp.sum(du.astype(F32), axis=0, keepdims=True)
            return c

        lax.fori_loop(0, CHUNKS * batches, mlp, 0)
        for j in range(CHUNKS):
            gd[j * D : (j + 1) * D, :] = gdt[:, j * D : (j + 1) * D].T

    if "f2b" in stages:
        ga[:, 3 * D :] = jnp.zeros((D, D), F32)
        heads[...] = jnp.zeros_like(heads)

        def turn(b, c):
            rs = rows_at(b)
            mid = m[b]
            live = iota((rows, D), 0) < live_of(b)
            out = jnp.where(live, mid + (y[b] + v(7)), 0.0)
            y[b] = out
            nr = heads.shape[0]
            pick = (places(b, iota((nr, 1), 0)) == iota((nr, rows), 1)).astype(BF)
            heads[...] += dg(pick, out.astype(BF), NN)
            xhat, r = norm_stats(mid)
            d2 = dh[b]
            gvec[5:6, :] += jnp.sum(d2 * xhat, axis=0, keepdims=True)
            gvec[6:7, :] += jnp.sum(d2, axis=0, keepdims=True)
            dm = dy[b] + norm_back(d2, v(5), xhat, r)
            dy[b] = dm
            d16 = dm.astype(BF)
            gvec[4:5, :] += jnp.sum(d16.astype(F32), axis=0, keepdims=True)
            ga[:, 3 * D :] += dg(o[rs, :], d16, TN)
            h2[rs, :] = dg(d16, wa[:, 3 * D :], NT).astype(BF)
            dh[b] = jnp.zeros((rows, D), F32)
            return c

        lax.fori_loop(0, batches, turn, 0)
        outs = [
            pltpu.make_async_copy(y.at[b], out_hbm.at[0, b], sem.at[b]) for b in range(batches)
        ]
        for c in outs:
            c.start()

    if "b1" in stages:
        for pair in range(PAIRS):
            c0 = pair * TILE

            def attend_back(b, c):
                rs = rows_at(b)
                y_k, y_v = m.at[0, :, 0:TILE], m.at[0, :, TILE : 2 * TILE]
                m[0, :, 0 : 2 * TILE] = jnp.zeros((rows, 2 * TILE), F32)
                for i, (q0, k0, lo, hi) in enumerate(layout):
                    qr = pl.ds(pl.multiple_of(b * rows + q0, 16), TILE)
                    kr = pl.ds(pl.multiple_of(b * rows + k0, 16), WIN)
                    wr = pl.ds(pl.multiple_of(k0, 16), WIN)
                    own = iota((TILE, TILE), 0) + q0
                    own = (own >= lo) & (own < hi)
                    do = h2[qr, pl.ds(c0, TILE)]
                    do = stack(jnp.where(own, do, jnp.zeros_like(do)))
                    q = stack(p[qr, pl.ds(c0, TILE)] * BF(HD**-0.5))
                    k = p[kr, pl.ds(D + c0, TILE)]
                    val = p[kr, pl.ds(2 * D + c0, TILE)]
                    a = att[b, pair, i]
                    af = a.astype(F32)
                    da = dg(val, do, NT)
                    ds = af * (da - jnp.sum(af * da, axis=0, keepdims=True))
                    ds = ds.astype(BF)
                    dq = (unstack(dg(ds, k, TN)) * HD**-0.5).astype(BF)
                    old = dp[qr, pl.ds(0, TILE)]
                    dp[qr, pl.ds(0, TILE)] = jnp.where(own, dq, old)
                    y_k[wr, :] += dg(ds, q, NN)
                    y_v[wr, :] += dg(a, do, NN)
                dp[rs, TILE : 2 * TILE] = y_k[...].astype(BF)
                dp[rs, 2 * TILE :] = y_v[...].astype(BF)
                w = jnp.concatenate(
                    [wa[:, s * D + c0 : s * D + c0 + TILE] for s in range(3)], axis=1
                )
                dh[b] += dg(dp[rs, :], w, NT)
                return c

            dp[:, 0:TILE] = jnp.zeros((batches * rows, TILE), BF)
            lax.fori_loop(0, batches, attend_back, 0)
            g = dg(h1t[...], dp[...], NN)
            sums = jnp.sum(dp[...].astype(F32), axis=0, keepdims=True)
            gvec[2:3, c0 : c0 + TILE] = sums[:, 0:TILE]
            gvec[3:4, c0 : c0 + TILE] = sums[:, 2 * TILE :]
            for s in range(3):
                ga[:, s * D + c0 : s * D + c0 + TILE] = g[:, s * TILE : (s + 1) * TILE]

    if "b2" in stages:
        for c in outs:
            c.wait()

        def last(b, c):
            xhat, r = norm_stats(x[b])
            d1 = dh[b]
            gvec[0:1, :] += jnp.sum(d1 * xhat, axis=0, keepdims=True)
            gvec[1:2, :] += jnp.sum(d1, axis=0, keepdims=True)
            y[b] = dy[b] + norm_back(d1, v(0), xhat, r)
            return c

        lax.fori_loop(0, batches, last, 0)
        outs = [
            pltpu.make_async_copy(y.at[b], ig_hbm.at[0, b], sem.at[b]) for b in range(batches)
        ]
        for c in outs:
            c.start()
        for c in outs:
            c.wait()


STAGES = ("f1", "at", "f1b", "f2", "f2b", "b1", "b2")


def run_main(lengths, routes, x, og, wa, wu, wd, vec, ret, capacity, owners, stages=STAGES):
    batches, rows = x.shape[1], x.shape[2]
    total = batches * rows
    vm = pl.BlockSpec(memory_space=pltpu.VMEM)
    sm = pl.BlockSpec(memory_space=pltpu.SMEM)
    anyspace = pl.BlockSpec(memory_space=pl.ANY)
    out_shape = (
        jax.ShapeDtypeStruct(x.shape, F32),
        jax.ShapeDtypeStruct(x.shape, F32),
        jax.ShapeDtypeStruct((D, 4 * D), F32),
        jax.ShapeDtypeStruct((D, FF), F32),
        jax.ShapeDtypeStruct((FF, D), F32),
        jax.ShapeDtypeStruct((16, D), F32),
        jax.ShapeDtypeStruct(ret.shape, F32),
    )
    act = pltpu.VMEM((total, D), BF)
    actt = pltpu.VMEM((D, total), BF)
    full = pltpu.VMEM((batches, rows, D), F32)
    scratch = [
        full, full, full, full, full,
        act, actt, pltpu.VMEM((total, 3 * D), BF),
        pltpu.VMEM((batches, PAIRS, 4, WIN, 2 * TILE), BF),
        act, act, actt, act, actt, act,
        pltpu.VMEM((D, FF), F32),
        pltpu.VMEM((4, WIN, 2 * TILE), F32),
        pltpu.SemaphoreType.DMA((2 * batches,)),
    ]
    return pl.pallas_call(
        functools.partial(main_kernel, capacity=capacity, owners=owners, stages=stages),
        out_shape=out_shape,
        in_specs=[sm, sm, anyspace, anyspace, vm, vm, vm, vm, vm],
        out_specs=(anyspace, anyspace, vm, vm, vm, vm, vm),
        scratch_shapes=scratch,
        compiler_params=pltpu.CompilerParams(vmem_limit_bytes=62 * 2**20),
        name="step_main",
    )(lengths, routes, x, og, wa, wu, wd, vec, ret)


def adam_update(master, moment_one, second, gradient, factor, step_rate, decay_rate):
    clipped = gradient * factor
    mean_new = BETA_ONE * moment_one + (1.0 - BETA_ONE) * clipped
    square_new = BETA_TWO * second + (1.0 - BETA_TWO) * clipped * clipped
    mean_hat = mean_new / (1.0 - BETA_ONE**STEP_NUM)
    square_hat = square_new / (1.0 - BETA_TWO**STEP_NUM)
    updated = master - step_rate * (
        mean_hat / (jnp.sqrt(square_hat) + ADAM_EPSILON) + decay_rate * master
    )
    return (updated, mean_new, square_new)


def pad_slots(a, owners, capacity, cap_pad):
    a = a.reshape(owners, capacity, D)
    return jnp.pad(a, ((0, 0), (0, cap_pad - capacity), (0, 0))).reshape(owners * cap_pad, D)


def local(tokens, out_grad, cls_grad, crop_lengths, cls_route, *state):
    masters, firsts, seconds = state[:5], state[5:10], state[10:15]
    axes = ("dp", "shard")
    owners = lax.axis_size("dp")
    capacity = cls_grad.shape[0] // owners
    cap_pad = -(-capacity // 8) * 8
    qkv, out, up, down, vector = (
        lax.all_gather(w.astype(BF), axes, axis=0, tiled=True) for w in masters
    )
    wa = jnp.concatenate([qkv.reshape(D, 3 * D), out.reshape(D, D)], axis=1)
    vec = jnp.pad(vector.astype(F32).reshape(12, D), ((0, 4), (0, 0)))
    returned = lax.all_to_all(
        cls_grad.reshape(owners, capacity, D).astype(BF), "dp", 0, 0, tiled=True
    )
    ret = pad_slots(returned.astype(F32), owners, capacity, cap_pad)
    block_out, input_grad, ga, gu, gd, gvec, heads = run_main(
        crop_lengths[0], cls_route[0], tokens, out_grad,
        wa, up.reshape(D, FF), down.reshape(FF, D), vec, ret, capacity, owners,
    )
    heads = heads.reshape(owners, cap_pad, D)[:, :capacity].astype(BF)
    cls_grouped = lax.all_to_all(heads, "dp", 0, 0, tiled=True).astype(F32)
    cls_grouped = cls_grouped.reshape(owners * capacity, D)
    grads = (ga[:, : 3 * D], ga[:, 3 * D :], gu, gd, gvec[:12])
    grads = [
        lax.psum_scatter(g.reshape(-1), axes, scatter_dimension=0, tiled=True) for g in grads
    ]
    grad_norm = jnp.sqrt(lax.psum(sum(jnp.sum(g * g) for g in grads), axes))
    factor = jnp.minimum(1.0, CLIP_LIMIT / grad_norm)
    rates = (RATE_MATRIX,) * 4 + (RATE_VECTOR,)
    decays = (WEIGHT_DECAY,) * 4 + (0.0,)
    new = [
        adam_update(masters[i], firsts[i], seconds[i], grads[i], factor, rates[i], decays[i])
        for i in range(5)
    ]
    return (block_out, cls_grouped, input_grad, grad_norm) + tuple(
        new[i][k] for k in range(3) for i in range(5)
    )


MESH = pl.DeviceIdType.MESH
CORE, Y, X, Z_LOW, Z_HIGH = 1, 2, 4, 8, 16
GATHER_ORDER = (
    (Z_LOW, Z_HIGH, X, Y, CORE),
    (Z_LOW, Z_HIGH, Y, X, CORE),
    (Z_LOW, Z_HIGH, X, Y, CORE),
)
BLOCK = 48
PART = 12
VM = pltpu.VMEM


class Place:
    def __init__(self):
        self.d = lax.axis_index("dp")
        self.s = lax.axis_index("shard")

    def bit(self, b):
        if b < 4:
            return (self.s // b) % 2
        return (self.d // (b // 4)) % 2

    def partner(self, b):
        step = 1 - 2 * self.bit(b)
        if b < 4:
            return (self.d, self.s + b * step)
        return (self.d + (b // 4) * step, self.s)

    def block(self, flips):
        d, s = self.d, self.s
        for b in (1, 2, 4, 8, 16):
            if (flips // b) % 2:
                step = 1 - 2 * self.bit(b)
                if b < 4:
                    s = s + b * step
                else:
                    d = d + (b // 4) * step
        return d, s


def choices(free):
    found = [0]
    for b in sorted(free):
        found = found + [c + b for c in found]
    return found


def block_of(ref, kind, d, s):
    if kind < 2:
        rows = pl.ds(pl.multiple_of(d * BLOCK, 16), BLOCK)
        return rows, pl.ds(pl.multiple_of(s * D, 128), D)
    return pl.ds(pl.multiple_of((d * 4 + s) * BLOCK, 16), BLOCK), pl.ds(0, D)


def greet(place, owners):
    barrier = pltpu.get_barrier_semaphore()
    for k in range(1, 4):
        pl.semaphore_signal(
            barrier, inc=1, device_id=(place.d, (place.s + k) % 4), device_id_type=MESH
        )
    for k in range(1, owners):
        pl.semaphore_signal(
            barrier, inc=1, device_id=((place.d + k) % owners, place.s), device_id_type=MESH
        )
    pl.semaphore_wait(barrier, 3 + owners - 1)


def send(src, dst, sems, n, device):
    copy = pltpu.make_async_remote_copy(
        src_ref=src, dst_ref=dst, send_sem=sems[0].at[n], recv_sem=sems[1].at[n],
        device_id=device, device_id_type=MESH,
    )
    copy.start()
    return copy


def vector_masks(place):
    span = 12 * D // 32
    first = (place.d * 4 + place.s) * span
    flat = iota((16, span), 1) + first
    row = iota((16, span), 0)
    rows = (flat >= row * D) & (flat < (row + 1) * D)
    col = iota((span, D), 1)
    at = iota((span, D), 0) + first
    cols = jnp.zeros((span, D), jnp.bool_)
    for k in range(12):
        cols = cols | (at - k * D == col)
    return rows, cols


def slot_map(shape, dim, capacity):
    padded, plain = iota(shape, dim), iota(shape, 1 - dim)
    owner = lax.shift_right_logical(padded, 3)
    inner = padded - owner * 8
    return ((inner < capacity) & (owner * capacity + inner == plain)).astype(BF)


def gather_kernel(
    wq, wo, wu_lin, wd_lin, vector, cls,
    wa, wu, wd, vec, ret,
    slab, got, vsend, vgot, csend, send_sem, recv_sem, *, owners, capacity
):
    place = Place()
    d, s = place.d, place.s
    sems = (send_sem, recv_sem)
    count = [0]
    started = []

    def go(src, dst, device):
        c = send(src, dst, sems, count[0], device)
        count[0] += 1
        started.append(c)
        return c

    for j in range(4):
        for t in range(3):
            c = 3 * j + t
            lanes = slice(t * 128, (t + 1) * 128)
            if j < 3:
                part = wq[pl.ds(c, PART, stride=9), :]
            else:
                part = wo[pl.ds(t, PART, stride=3), :]
            slab[j, 0, 0:PART, lanes] = part.astype(BF)
            slab[j, 1, 0:PART, lanes] = wu_lin[pl.ds(c, PART, stride=12), :].astype(BF)
    rows, _ = block_of(wd, 2, d, s)
    for t in range(3):
        wd[rows, t * 128 : (t + 1) * 128] = wd_lin[pl.ds(t, BLOCK, stride=3), :].astype(BF)
    csend[...] = dg(slot_map((csend.shape[0], cls.shape[0]), 0, capacity), cls[...].astype(BF), NN)
    vrows, vcols = vector_masks(place)
    mine = jnp.where(vrows, vector[...], 0.0).astype(BF)
    vsend[0] = dg(mine, vcols.astype(BF), NN).astype(BF)

    greet(place, owners)

    first = []
    for k in range(1, 4):
        j = (s + k) % 4
        first.append(go(slab.at[j], got.at[s], (d, j)))
    got[s] = slab[s]
    exchange = []
    ret[pl.ds(pl.multiple_of(d * 8, 8), 8), :] = csend[pl.ds(pl.multiple_of(d * 8, 8), 8), :]
    for k in range(1, owners):
        o = (d + k) % owners
        exchange.append(
            go(
                csend.at[pl.ds(pl.multiple_of(o * 8, 8), 8)],
                ret.at[pl.ds(pl.multiple_of(d * 8, 8), 8)],
                (o, s),
            )
        )
    pending = [[], [], []]
    vpending = None

    def stage(kind, k):
        ref = (wa, wu, wd)[kind]
        order = GATHER_ORDER[kind]
        for c in pending[kind]:
            c.wait_recv()
        pending[kind] = []
        if k == 5:
            return
        to = place.partner(order[k])
        free = order[:k]
        if kind < 2 and all(b in free for b in (X, Z_LOW, Z_HIGH)):
            for c in choices([b for b in free if b < 4]):
                _, bs = place.block(c)
                at = ref.at[:, pl.ds(pl.multiple_of(bs * D, 128), D)]
                pending[kind].append(go(at, at, to))
            return
        for c in choices(free):
            bd, bs = place.block(c)
            r, cc = block_of(ref, kind, bd, bs)
            at = ref.at[r, cc]
            pending[kind].append(go(at, at, to))

    for k in range(6):
        if vpending is not None:
            vpending.wait_recv()
            total = vsend[k - 1] + vgot[k - 1]
            if k < 5:
                vsend[k] = total
            else:
                vec[...] = total.astype(F32)
        if k < 5:
            vpending = go(vsend.at[k], vgot.at[k], place.partner(GATHER_ORDER[0][k]))
        if k == 0:
            stage(2, 0)
            for c in first:
                c.wait_recv()
            for kind, ref in enumerate((wa, wu)):
                full = jnp.concatenate(
                    [got[j, kind].astype(F32)[0:PART] for j in range(4)], axis=0
                )
                r, cc = block_of(ref, kind, d, s)
                ref[r, cc] = full.astype(BF)
            stage(0, 0)
            stage(1, 0)
        else:
            for kind in range(3):
                stage(kind, k)
    for c in exchange:
        c.wait_recv()
    for c in started:
        c.wait_send()


def run_gather(masters, cls, owners, capacity):
    qkv, out, up, down, vector = masters
    ins = [w.reshape(-1, 128) for w in (qkv, out, up, down)]
    slots = owners * 8
    vm = pl.BlockSpec(memory_space=VM)
    return pl.pallas_call(
        functools.partial(gather_kernel, owners=owners, capacity=capacity),
        out_shape=(
            jax.ShapeDtypeStruct((D, 4 * D), BF),
            jax.ShapeDtypeStruct((D, FF), BF),
            jax.ShapeDtypeStruct((FF, D), BF),
            jax.ShapeDtypeStruct((16, D), F32),
            jax.ShapeDtypeStruct((slots, D), F32),
        ),
        in_specs=[vm] * 6,
        out_specs=(vm,) * 5,
        scratch_shapes=[
            VM((4, 2, 16, D), BF), VM((4, 2, 16, D), BF), VM((5, 16, D), BF), VM((5, 16, D), BF),
            VM((slots, D), F32),
            pltpu.SemaphoreType.DMA((128,)), pltpu.SemaphoreType.DMA((128,)),
        ],
        compiler_params=pltpu.CompilerParams(
            collective_id=1, has_side_effects=True, vmem_limit_bytes=32 * 2**20
        ),
        name="gather_weights",
    )(*ins, vector.reshape(1, -1), cls)


def adam_terms(master, first, second, gradient, factor, rate, decay):
    clipped = gradient * factor
    mean = BETA_ONE * first + (1.0 - BETA_ONE) * clipped
    square = BETA_TWO * second + (1.0 - BETA_TWO) * clipped * clipped
    mean_hat = mean / (1.0 - BETA_ONE**STEP_NUM)
    square_hat = square / (1.0 - BETA_TWO**STEP_NUM)
    step = mean_hat / (jnp.sqrt(square_hat) + ADAM_EPSILON)
    return master - rate * (step + decay * master), mean, square


REDUCE_ORDER = (
    (CORE, Y, X, Z_HIGH, Z_LOW),
    (CORE, X, Y, Z_HIGH, Z_LOW),
    (CORE, Y, X, Z_HIGH, Z_LOW),
)
OFFSETS = (0, 16, 24, 28, 30)


def update_kernel(*refs, owners, capacity):
    ga_in, gu_in, gd_in, gvec, heads = refs[:5]
    state = refs[5:20]
    cls_out, norm_out = refs[20:22]
    results = refs[22:37]
    acc, sbuf, rbuf, part_send, part_got, lin_q, lin_o, lin_u, lin_d = refs[37:46]
    cgot, vacc, vgot, square_buf, square_got, total_buf, total_got, send_sem, recv_sem = refs[46:]
    place = Place()
    d, s = place.d, place.s
    sems = (send_sem, recv_sem)
    count = [0]
    started = []

    def go(src, dst, device):
        c = send(src, dst, sems, count[0], device)
        count[0] += 1
        started.append(c)
        return c

    greet(place, owners)
    exchange = []
    mine = pl.ds(pl.multiple_of(d * 8, 8), 8)
    cgot[mine, :] = heads[mine, :]
    for k in range(1, owners):
        o = (d + k) % owners
        exchange.append(
            go(heads.at[pl.ds(pl.multiple_of(o * 8, 8), 8)], cgot.at[mine], (o, s))
        )
    sources = (ga_in, gu_in, gd_in)
    pending = [None, None, None]
    vpending = None
    vacc[0] = gvec[...]

    def stage(kind, k):
        order = REDUCE_ORDER[kind]

        def partial(c):
            if k == 0:
                bd, bs = place.block(c)
                return sources[kind][block_of(sources[kind], kind, bd, bs)]
            slot = OFFSETS[k - 1] + choices(order[k:]).index(c)
            if k == 1:
                bd, bs = place.block(c)
                own = sources[kind][block_of(sources[kind], kind, bd, bs)]
            else:
                own = acc[kind, OFFSETS[k - 2] + choices(order[k - 1 :]).index(c)]
            total = own + rbuf[kind, slot].astype(F32)
            acc[kind, slot] = total
            return total

        if k > 0:
            pending[kind].wait_recv()
        if k == 5:
            partial(0)
            return
        rest = order[k + 1 :]
        for n, c in enumerate(choices(rest)):
            sbuf[kind, n + OFFSETS[k]] = partial(c + order[k]).astype(BF)
        span = pl.ds(OFFSETS[k], 2 ** (4 - k))
        pending[kind] = go(
            sbuf.at[kind, span], rbuf.at[kind, span], place.partner(order[k])
        )
        if k > 0:
            for c in choices(rest):
                partial(c)

    for k in range(6):
        if vpending is not None:
            vpending.wait_recv()
            vacc[k] = vacc[k - 1] + vgot[k - 1]
        if k < 5:
            vpending = go(vacc.at[k], vgot.at[k], place.partner(REDUCE_ORDER[0][k]))
        for kind in (1, 2, 0):
            stage(kind, k)

    first = []
    for kind in range(2):
        full = acc[kind, 30]
        for j in range(4):
            part_send[j, kind, 0:PART] = full[j * PART : (j + 1) * PART]
    for k in range(1, 4):
        j = (s + k) % 4
        first.append(go(part_send.at[j], part_got.at[s], (d, j)))
    part_got[s] = part_send[s]
    for t in range(3):
        lin_d[pl.ds(t, BLOCK, stride=3), :] = acc[2, 30, :, t * 128 : (t + 1) * 128]
    for c in exchange:
        c.wait_recv()
    pick = slot_map((cls_out.shape[0], cgot.shape[0]), 1, capacity)
    cls_out[...] = dg(pick, cgot[...].astype(BF), NN)
    vector_grad = vacc[5]
    vrows, vcols = vector_masks(place)
    mine_v = lax.dot_general(
        vector_grad, vcols.astype(F32), NT, precision=lax.Precision.HIGHEST,
        preferred_element_type=F32,
    )
    vector_mine = jnp.sum(jnp.where(vrows, mine_v, 0.0), axis=0, keepdims=True)
    for c in first:
        c.wait_recv()
    for j in range(4):
        for t in range(3):
            c = 3 * j + t
            lanes = slice(t * 128, (t + 1) * 128)
            if j < 3:
                lin_q[pl.ds(c, PART, stride=9), :] = part_got[j, 0, 0:PART, lanes]
            else:
                lin_o[pl.ds(t, PART, stride=3), :] = part_got[j, 0, 0:PART, lanes]
            lin_u[pl.ds(c, PART, stride=12), :] = part_got[j, 1, 0:PART, lanes]
    grads = [lin_q[...], lin_o[...], lin_u[...], lin_d[...]]
    squares = [jnp.sum(g * g, axis=0, keepdims=True) for g in grads]
    squares = squares[0] + squares[1] + squares[2] + squares[3]
    square_buf[...] = jnp.broadcast_to(squares, (8, 128))
    own = [go(square_buf, square_got.at[s], (d, (s + k) % 4)) for k in range(1, 4)]
    square_got[s] = square_buf[...]
    for c in own:
        c.wait_recv()
    total_buf[...] = (square_got[0] + square_got[1]) + (square_got[2] + square_got[3])
    own = [go(total_buf, total_got.at[d], ((d + k) % owners, s)) for k in range(1, owners)]
    total_got[d] = total_buf[...]
    for c in own:
        c.wait_recv()
    total = total_got[0]
    for k in range(1, owners):
        total = total + total_got[k]
    total = jnp.sum(total[0:1, :], axis=1, keepdims=True)
    vector_square = jnp.sum(vector_grad * vector_grad, axis=0, keepdims=True)
    total = total + jnp.sum(vector_square, axis=1, keepdims=True)
    norm = jnp.sqrt(total)
    norm_out[...] = norm
    factor = jnp.minimum(1.0, CLIP_LIMIT / norm)
    grads.append(vector_mine)
    for i in range(5):
        rate, decay = (RATE_VECTOR, 0.0) if i == 4 else (RATE_MATRIX, WEIGHT_DECAY)
        new = adam_terms(
            state[i][...], state[5 + i][...], state[10 + i][...], grads[i], factor, rate, decay
        )
        for k in range(3):
            results[5 * k + i][...] = new[k]
    for c in started:
        c.wait_send()


def run_update(ga, gu, gd, gvec, heads, state, owners, capacity):
    flat = [w.reshape(1, -1) if i % 5 == 4 else w.reshape(-1, 128) for i, w in enumerate(state)]
    vm = pl.BlockSpec(memory_space=VM)
    out_shape = (
        jax.ShapeDtypeStruct((owners * capacity, D), F32), jax.ShapeDtypeStruct((1, 1), F32),
    ) + tuple(jax.ShapeDtypeStruct(w.shape, F32) for w in flat)
    sizes = [w.shape for w in flat[:4]]
    scratch = [
        VM((3, 31, BLOCK, D), F32), VM((3, 31, BLOCK, D), BF), VM((3, 31, BLOCK, D), BF),
        VM((4, 2, 16, D), F32), VM((4, 2, 16, D), F32),
    ] + [VM(z, F32) for z in sizes] + [
        VM(heads.shape, F32), VM((6, 16, D), F32), VM((5, 16, D), F32),
        VM((8, 128), F32), VM((4, 8, 128), F32), VM((8, 128), F32), VM((owners, 8, 128), F32),
        pltpu.SemaphoreType.DMA((64,)), pltpu.SemaphoreType.DMA((64,)),
    ]
    return pl.pallas_call(
        functools.partial(update_kernel, owners=owners, capacity=capacity),
        out_shape=out_shape,
        in_specs=[vm] * 20,
        out_specs=(vm,) * 17,
        scratch_shapes=scratch,
        compiler_params=pltpu.CompilerParams(
            collective_id=2, has_side_effects=True, vmem_limit_bytes=56 * 2**20
        ),
        name="reduce_update",
    )(ga, gu, gd, gvec, heads, *flat)


def local_fast(tokens, out_grad, cls_grad, crop_lengths, cls_route, *state):
    owners = lax.axis_size("dp")
    capacity = cls_grad.shape[0] // owners
    wa, wu, wd, vec, ret = run_gather(state[:5], cls_grad, owners, capacity)
    block_out, input_grad, ga, gu, gd, gvec, heads = run_main(
        crop_lengths[0], cls_route[0], tokens, out_grad, wa, wu, wd, vec, ret, capacity, owners
    )
    new = run_update(ga, gu, gd, gvec, heads, state, owners, capacity)
    rest = tuple(w.reshape(-1) for w in new[2:])
    return (block_out, new[0], input_grad, new[1].reshape(())) + rest


def solution(mesh):
    spread = ("dp", "shard")
    in_specs = (
        P(spread, None, None, None), P(spread, None, None, None), P(spread, None),
        P(spread, None, None), P(spread, None, None),
    ) + (P(spread),) * 15
    out_specs = (
        P(spread, None, None, None), P(spread, None), P(spread, None, None, None), P(),
    ) + (P(spread),) * 15
    fast = mesh.shape["shard"] == 4 and mesh.shape["dp"] == 8
    body = local_fast if fast else local
    return jax.shard_map(body, mesh=mesh, in_specs=in_specs, out_specs=out_specs, check_vma=False)
```

```python
import functools

import jax
import jax.numpy as jnp
from jax import lax
from jax.experimental import pallas as pl
from jax.experimental.pallas import tpu as pltpu
from jax.sharding import PartitionSpec as P

D = 384
H = 6
HD = 64
FF = 1536
STEP_NUM = 10
LG = 197
LF = 37

NORM_EPSILON = 1e-06
BETA_ONE = 0.9
BETA_TWO = 0.999
ADAM_EPSILON = 1e-08
RATE_MATRIX = 0.05
RATE_VECTOR = 0.3
WEIGHT_DECAY = 0.05
CLIP_LIMIT = 1.0
MASK_VALUE = -1e30

BF = jnp.bfloat16
F32 = jnp.float32
NN = (((1,), (0,)), ((), ()))
NT = (((1,), (1,)), ((), ()))
TN = (((0,), (0,)), ((), ()))
PAIRS = H // 2
CHUNKS = FF // D
TILE = 128
WIN = 256


def dg(a, b, dims):
    return lax.dot_general(a, b, dims, preferred_element_type=F32)


def iota(shape, dim):
    return lax.broadcasted_iota(jnp.int32, shape, dim)


def tiles(is_global):
    focal = ((0, 0, 0, 128), (128, 64, 128, 256), (256, 192, 256, 384), (384, 256, 384, 512))
    whole = ((0, 0, 0, 128), (80, 0, 128, 197), (192, 192, 197, 320), (272, 192, 320, 394))
    return [
        tuple(jnp.where(is_global, w, f) for w, f in zip(whole[i], focal[i])) for i in range(4)
    ]


def norm_stats(v):
    mean = jnp.mean(v, axis=-1, keepdims=True)
    c = v - mean
    var = jnp.mean(c * c, axis=-1, keepdims=True)
    r = lax.rsqrt(var + NORM_EPSILON)
    return c * r, r


def norm_back(dh, gain, xhat, r):
    d = dh * gain
    m1 = jnp.mean(d, axis=-1, keepdims=True)
    m2 = jnp.mean(d * xhat, axis=-1, keepdims=True)
    return (d - m1 - xhat * m2) * r


def gelu_parts(u):
    cdf = 0.5 + 0.5 * lax.erf(u * 0.7071067811865476)
    pdf = jnp.exp(u * u * -0.5) * 0.3989422804014327
    return u * cdf, cdf + u * pdf


def main_kernel(
    lengths, routes, x_hbm, og_hbm, wa, wu, wd, vec, ret,
    out_hbm, ig_hbm, ga, gu, gd, gvec, heads,
    x, dy, y, m, dh, h1, h1t, p, att, o, h2, h2t, dy16, dy16t, dp, gdt, bias, sem,
    *, capacity, owners, stages
):
    batches, rows = x.shape[0], x.shape[1]
    slots = lengths.shape[1]
    cap_pad = ret.shape[0] // owners
    is_global = lax.axis_index("dp") % 2 == 0
    length = jnp.where(is_global, LG, LF)
    layout = tiles(is_global)

    copies = [
        pltpu.make_async_copy(x_hbm.at[0, b], x.at[b], sem.at[b]) for b in range(batches)
    ] + [
        pltpu.make_async_copy(og_hbm.at[0, b], dy.at[b], sem.at[batches + b])
        for b in range(batches)
    ]
    for c in copies:
        c.start()

    def segment_of(t):
        return jnp.where(
            is_global,
            (t >= LG).astype(jnp.int32) + (t >= 2 * LG).astype(jnp.int32),
            lax.shift_right_logical(t * 1772, 16),
        )

    for i, (q0, k0, lo, hi) in enumerate(layout):
        keys = segment_of(iota((WIN, TILE), 0) + k0)
        queries = segment_of(iota((WIN, TILE), 1) + q0)
        mask = jnp.where(keys == queries, 0.0, MASK_VALUE).astype(F32)
        bias[i, :, :TILE] = mask
        bias[i, :, TILE:] = mask

    def v(row):
        return vec[row : row + 1, :]

    low_half = iota((TILE, TILE), 1) < HD

    def stack(t):
        z = jnp.zeros_like(t)
        return jnp.concatenate([jnp.where(low_half, t, z), jnp.where(low_half, z, t)], axis=0)

    def unstack(t):
        return jnp.where(low_half, t[:TILE], t[TILE:])

    def rows_at(b):
        return pl.ds(pl.multiple_of(b * rows, rows), rows)

    gvec[...] = jnp.zeros_like(gvec)
    if "f1" in stages:
        for b in range(batches):
            copies[b].wait()

        def attend(b, c):
            rs = rows_at(b)
            xhat, _ = norm_stats(x[b])
            h = (xhat * v(0) + v(1)).astype(BF)
            h1[rs, :] = h
            h1t[:, rs] = h.T
            p[rs, 0:D] = (dg(h, wa[:, 0:D], NN) + v(2)).astype(BF)
            p[rs, D : 2 * D] = dg(h, wa[:, D : 2 * D], NN).astype(BF)
            p[rs, 2 * D : 3 * D] = (dg(h, wa[:, 2 * D : 3 * D], NN) + v(3)).astype(BF)
            for pair in range(PAIRS if "at" in stages else 0):
                c0 = pair * TILE
                for i, (q0, k0, lo, hi) in enumerate(layout):
                    qr = pl.ds(pl.multiple_of(b * rows + q0, 16), TILE)
                    kr = pl.ds(pl.multiple_of(b * rows + k0, 16), WIN)
                    q = stack(p[qr, pl.ds(c0, TILE)] * BF(HD**-0.5))
                    k = p[kr, pl.ds(D + c0, TILE)]
                    val = p[kr, pl.ds(2 * D + c0, TILE)]
                    s = dg(k, q, NT) + bias[i]
                    e = jnp.exp(s - jnp.max(s, axis=0, keepdims=True))
                    a = (e * (1.0 / jnp.sum(e, axis=0, keepdims=True))).astype(BF)
                    att[b, pair, i] = a
                    r = unstack(dg(a, val, TN)).astype(BF)
                    own = iota((TILE, TILE), 0) + q0
                    own = (own >= lo) & (own < hi)
                    old = o[qr, pl.ds(c0, TILE)]
                    o[qr, pl.ds(c0, TILE)] = jnp.where(own, r, old)
            return c

        o[...] = jnp.zeros_like(o)
        lax.fori_loop(0, batches, attend, 0)

    def live_of(b):
        n = lengths[b, 0]
        for k in range(1, slots):
            n = n + lengths[b, k]
        return n

    def places(b, r):
        spot = jnp.full(r.shape, -1, jnp.int32)
        for k in range(slots):
            route = routes[b, k]
            padded = (route // capacity) * cap_pad + route % capacity
            padded = jnp.where(route >= 0, padded, -1)
            spot = jnp.where(r == padded, k * length, spot)
        return spot

    if "f1b" in stages:
        for b in range(batches):
            copies[batches + b].wait()

        def middle(b, c):
            rs = rows_at(b)
            mid = x[b] + (dg(o[rs, :], wa[:, 3 * D :], NN) + v(4))
            m[b] = mid
            xhat, _ = norm_stats(mid)
            h = (xhat * v(5) + v(6)).astype(BF)
            h2[rs, :] = h
            h2t[:, rs] = h.T
            nr = ret.shape[0]
            pick = (iota((rows, nr), 0) == places(b, iota((1, nr), 1))).astype(BF)
            live = iota((rows, D), 0) < live_of(b)
            g = dy[b] + dg(pick, ret[...].astype(BF), NN)
            g = jnp.where(live, g, 0.0)
            dy[b] = g
            g16 = g.astype(BF)
            dy16[rs, :] = g16
            dy16t[:, rs] = g16.T
            gvec[7:8, :] += jnp.sum(g16.astype(F32), axis=0, keepdims=True)
            y[b] = jnp.zeros((rows, D), F32)
            dh[b] = jnp.zeros((rows, D), F32)
            return c

        lax.fori_loop(0, batches, middle, 0)

    if "f2" in stages:
        gu[...] = jnp.zeros_like(gu)
        gdt[...] = jnp.zeros_like(gdt)

        def mlp(t, c):
            j, b = t // batches, t % batches
            rs = rows_at(b)
            cs = pl.ds(pl.multiple_of(j * D, D), D)
            u = dg(h2[rs, :], wu[:, cs], NN) + vec[pl.ds(8 + j, 1), :]
            g, slope = gelu_parts(u)
            g = g.astype(BF)
            y[b] += dg(g, wd[cs, :], NN)
            gdt[:, cs] += dg(dy16t[:, rs], g, NN)
            du = (dg(dy16[rs, :], wd[cs, :], NT) * slope).astype(BF)
            gu[:, cs] += dg(h2t[:, rs], du, NN)
            dh[b] += dg(du, wu[:, cs], NT)
            gvec[pl.ds(8 + j, 1), :] += jnp.sum(du.astype(F32), axis=0, keepdims=True)
            return c

        lax.fori_loop(0, CHUNKS * batches, mlp, 0)
        for j in range(CHUNKS):
            gd[j * D : (j + 1) * D, :] = gdt[:, j * D : (j + 1) * D].T

    if "f2b" in stages:
        ga[:, 3 * D :] = jnp.zeros((D, D), F32)
        heads[...] = jnp.zeros_like(heads)

        def turn(b, c):
            rs = rows_at(b)
            mid = m[b]
            live = iota((rows, D), 0) < live_of(b)
            out = jnp.where(live, mid + (y[b] + v(7)), 0.0)
            y[b] = out
            nr = heads.shape[0]
            pick = (places(b, iota((nr, 1), 0)) == iota((nr, rows), 1)).astype(BF)
            heads[...] += dg(pick, out.astype(BF), NN)
            xhat, r = norm_stats(mid)
            d2 = dh[b]
            gvec[5:6, :] += jnp.sum(d2 * xhat, axis=0, keepdims=True)
            gvec[6:7, :] += jnp.sum(d2, axis=0, keepdims=True)
            dm = dy[b] + norm_back(d2, v(5), xhat, r)
            dy[b] = dm
            d16 = dm.astype(BF)
            gvec[4:5, :] += jnp.sum(d16.astype(F32), axis=0, keepdims=True)
            ga[:, 3 * D :] += dg(o[rs, :], d16, TN)
            h2[rs, :] = dg(d16, wa[:, 3 * D :], NT).astype(BF)
            dh[b] = jnp.zeros((rows, D), F32)
            return c

        lax.fori_loop(0, batches, turn, 0)
        outs = [
            pltpu.make_async_copy(y.at[b], out_hbm.at[0, b], sem.at[b]) for b in range(batches)
        ]
        for c in outs:
            c.start()

    if "b1" in stages:
        for pair in range(PAIRS):
            c0 = pair * TILE

            def attend_back(b, c):
                rs = rows_at(b)
                y_k, y_v = m.at[0, :, 0:TILE], m.at[0, :, TILE : 2 * TILE]
                m[0, :, 0 : 2 * TILE] = jnp.zeros((rows, 2 * TILE), F32)
                for i, (q0, k0, lo, hi) in enumerate(layout):
                    qr = pl.ds(pl.multiple_of(b * rows + q0, 16), TILE)
                    kr = pl.ds(pl.multiple_of(b * rows + k0, 16), WIN)
                    wr = pl.ds(pl.multiple_of(k0, 16), WIN)
                    own = iota((TILE, TILE), 0) + q0
                    own = (own >= lo) & (own < hi)
                    do = h2[qr, pl.ds(c0, TILE)]
                    do = stack(jnp.where(own, do, jnp.zeros_like(do)))
                    q = stack(p[qr, pl.ds(c0, TILE)] * BF(HD**-0.5))
                    k = p[kr, pl.ds(D + c0, TILE)]
                    val = p[kr, pl.ds(2 * D + c0, TILE)]
                    a = att[b, pair, i]
                    af = a.astype(F32)
                    da = dg(val, do, NT)
                    ds = af * (da - jnp.sum(af * da, axis=0, keepdims=True))
                    ds = ds.astype(BF)
                    dq = (unstack(dg(ds, k, TN)) * HD**-0.5).astype(BF)
                    old = dp[qr, pl.ds(0, TILE)]
                    dp[qr, pl.ds(0, TILE)] = jnp.where(own, dq, old)
                    y_k[wr, :] += dg(ds, q, NN)
                    y_v[wr, :] += dg(a, do, NN)
                dp[rs, TILE : 2 * TILE] = y_k[...].astype(BF)
                dp[rs, 2 * TILE :] = y_v[...].astype(BF)
                w = jnp.concatenate(
                    [wa[:, s * D + c0 : s * D + c0 + TILE] for s in range(3)], axis=1
                )
                dh[b] += dg(dp[rs, :], w, NT)
                return c

            dp[:, 0:TILE] = jnp.zeros((batches * rows, TILE), BF)
            lax.fori_loop(0, batches, attend_back, 0)
            g = dg(h1t[...], dp[...], NN)
            sums = jnp.sum(dp[...].astype(F32), axis=0, keepdims=True)
            gvec[2:3, c0 : c0 + TILE] = sums[:, 0:TILE]
            gvec[3:4, c0 : c0 + TILE] = sums[:, 2 * TILE :]
            for s in range(3):
                ga[:, s * D + c0 : s * D + c0 + TILE] = g[:, s * TILE : (s + 1) * TILE]

    if "b2" in stages:
        for c in outs:
            c.wait()

        def last(b, c):
            xhat, r = norm_stats(x[b])
            d1 = dh[b]
            gvec[0:1, :] += jnp.sum(d1 * xhat, axis=0, keepdims=True)
            gvec[1:2, :] += jnp.sum(d1, axis=0, keepdims=True)
            y[b] = dy[b] + norm_back(d1, v(0), xhat, r)
            return c

        lax.fori_loop(0, batches, last, 0)
        outs = [
            pltpu.make_async_copy(y.at[b], ig_hbm.at[0, b], sem.at[b]) for b in range(batches)
        ]
        for c in outs:
            c.start()
        for c in outs:
            c.wait()


STAGES = ("f1", "at", "f1b", "f2", "f2b", "b1", "b2")


def run_main(lengths, routes, x, og, wa, wu, wd, vec, ret, capacity, owners, stages=STAGES):
    batches, rows = x.shape[1], x.shape[2]
    total = batches * rows
    vm = pl.BlockSpec(memory_space=pltpu.VMEM)
    sm = pl.BlockSpec(memory_space=pltpu.SMEM)
    anyspace = pl.BlockSpec(memory_space=pl.ANY)
    out_shape = (
        jax.ShapeDtypeStruct(x.shape, F32),
        jax.ShapeDtypeStruct(x.shape, F32),
        jax.ShapeDtypeStruct((D, 4 * D), F32),
        jax.ShapeDtypeStruct((D, FF), F32),
        jax.ShapeDtypeStruct((FF, D), F32),
        jax.ShapeDtypeStruct((16, D), F32),
        jax.ShapeDtypeStruct(ret.shape, F32),
    )
    act = pltpu.VMEM((total, D), BF)
    actt = pltpu.VMEM((D, total), BF)
    full = pltpu.VMEM((batches, rows, D), F32)
    scratch = [
        full, full, full, full, full,
        act, actt, pltpu.VMEM((total, 3 * D), BF),
        pltpu.VMEM((batches, PAIRS, 4, WIN, 2 * TILE), BF),
        act, act, actt, act, actt, act,
        pltpu.VMEM((D, FF), F32),
        pltpu.VMEM((4, WIN, 2 * TILE), F32),
        pltpu.SemaphoreType.DMA((2 * batches,)),
    ]
    return pl.pallas_call(
        functools.partial(main_kernel, capacity=capacity, owners=owners, stages=stages),
        out_shape=out_shape,
        in_specs=[sm, sm, anyspace, anyspace, vm, vm, vm, vm, vm],
        out_specs=(anyspace, anyspace, vm, vm, vm, vm, vm),
        scratch_shapes=scratch,
        compiler_params=pltpu.CompilerParams(vmem_limit_bytes=62 * 2**20),
        name="step_main",
    )(lengths, routes, x, og, wa, wu, wd, vec, ret)


def adam_update(master, moment_one, second, gradient, factor, step_rate, decay_rate):
    clipped = gradient * factor
    mean_new = BETA_ONE * moment_one + (1.0 - BETA_ONE) * clipped
    square_new = BETA_TWO * second + (1.0 - BETA_TWO) * clipped * clipped
    mean_hat = mean_new / (1.0 - BETA_ONE**STEP_NUM)
    square_hat = square_new / (1.0 - BETA_TWO**STEP_NUM)
    updated = master - step_rate * (
        mean_hat / (jnp.sqrt(square_hat) + ADAM_EPSILON) + decay_rate * master
    )
    return (updated, mean_new, square_new)


def pad_slots(a, owners, capacity, cap_pad):
    a = a.reshape(owners, capacity, D)
    return jnp.pad(a, ((0, 0), (0, cap_pad - capacity), (0, 0))).reshape(owners * cap_pad, D)


def local(tokens, out_grad, cls_grad, crop_lengths, cls_route, *state):
    masters, firsts, seconds = state[:5], state[5:10], state[10:15]
    axes = ("dp", "shard")
    owners = lax.axis_size("dp")
    capacity = cls_grad.shape[0] // owners
    cap_pad = -(-capacity // 8) * 8
    qkv, out, up, down, vector = (
        lax.all_gather(w.astype(BF), axes, axis=0, tiled=True) for w in masters
    )
    wa = jnp.concatenate([qkv.reshape(D, 3 * D), out.reshape(D, D)], axis=1)
    vec = jnp.pad(vector.astype(F32).reshape(12, D), ((0, 4), (0, 0)))
    returned = lax.all_to_all(
        cls_grad.reshape(owners, capacity, D).astype(BF), "dp", 0, 0, tiled=True
    )
    ret = pad_slots(returned.astype(F32), owners, capacity, cap_pad)
    block_out, input_grad, ga, gu, gd, gvec, heads = run_main(
        crop_lengths[0], cls_route[0], tokens, out_grad,
        wa, up.reshape(D, FF), down.reshape(FF, D), vec, ret, capacity, owners,
    )
    heads = heads.reshape(owners, cap_pad, D)[:, :capacity].astype(BF)
    cls_grouped = lax.all_to_all(heads, "dp", 0, 0, tiled=True).astype(F32)
    cls_grouped = cls_grouped.reshape(owners * capacity, D)
    grads = (ga[:, : 3 * D], ga[:, 3 * D :], gu, gd, gvec[:12])
    grads = [
        lax.psum_scatter(g.reshape(-1), axes, scatter_dimension=0, tiled=True) for g in grads
    ]
    grad_norm = jnp.sqrt(lax.psum(sum(jnp.sum(g * g) for g in grads), axes))
    factor = jnp.minimum(1.0, CLIP_LIMIT / grad_norm)
    rates = (RATE_MATRIX,) * 4 + (RATE_VECTOR,)
    decays = (WEIGHT_DECAY,) * 4 + (0.0,)
    new = [
        adam_update(masters[i], firsts[i], seconds[i], grads[i], factor, rates[i], decays[i])
        for i in range(5)
    ]
    return (block_out, cls_grouped, input_grad, grad_norm) + tuple(
        new[i][k] for k in range(3) for i in range(5)
    )


MESH = pl.DeviceIdType.MESH
VM = pltpu.VMEM
CORE, Y, X, Z_LOW, Z_HIGH = 1, 2, 4, 8, 16
PLANE, LINE = X + Y, Z_LOW + Z_HIGH
BLOCK = 48
PART = 12
GATHERS = (
    (0, 0, 256, (LINE, PLANE, CORE)),
    (0, 256, 128, (PLANE, LINE, CORE)),
    (1, 0, 256, (LINE, PLANE, CORE)),
    (1, 256, 128, (PLANE, LINE, CORE)),
    (2, 0, 256, (LINE, PLANE, CORE)),
    (2, 256, 128, (PLANE, LINE, CORE)),
)
REDUCES = (
    (1, 0, 256, (CORE, PLANE, LINE)),
    (1, 256, 128, (CORE, LINE, PLANE)),
    (2, 0, 256, (CORE, PLANE, LINE)),
    (2, 256, 128, (CORE, LINE, PLANE)),
    (0, 0, 128, (CORE, PLANE, LINE)),
    (0, 128, 128, (CORE, PLANE, LINE)),
    (0, 256, 128, (CORE, PLANE, LINE)),
)
VECTOR_ORDER = (LINE, PLANE, CORE)


def subsets(bits):
    found = [0]
    for b in (1, 2, 4, 8, 16):
        if bits & b:
            found = found + [c + b for c in found]
    return found


class Place:
    def __init__(self):
        self.d = lax.axis_index("dp")
        self.s = lax.axis_index("shard")

    def away(self, flips):
        d, s = self.d, self.s
        for b in (1, 2):
            if flips & b:
                s = s + b * (1 - 2 * ((self.s // b) % 2))
        for b in (4, 8, 16):
            if flips & b:
                d = d + (b // 4) * (1 - 2 * ((self.d // (b // 4)) % 2))
        return d, s


def block_at(kind, where, lane, width):
    d, s = where
    if kind < 2:
        rows = pl.ds(pl.multiple_of(d * BLOCK, 16), BLOCK)
        return rows, pl.ds(pl.multiple_of(s * D + lane, 128), width)
    return pl.ds(pl.multiple_of((d * 4 + s) * BLOCK, 16), BLOCK), pl.ds(lane, width)


def vector_masks(place):
    span = 12 * D // 32
    first = (place.d * 4 + place.s) * span
    flat = iota((16, span), 1) + first
    row = iota((16, span), 0)
    rows = (flat >= row * D) & (flat < (row + 1) * D)
    col = iota((span, D), 1)
    at = iota((span, D), 0) + first
    cols = jnp.zeros((span, D), jnp.bool_)
    for k in range(12):
        cols = cols | (at - k * D == col)
    return rows, cols


def slot_map(shape, dim, capacity):
    padded, plain = iota(shape, dim), iota(shape, 1 - dim)
    owner = lax.shift_right_logical(padded, 3)
    inner = padded - owner * 8
    return ((inner < capacity) & (owner * capacity + inner == plain)).astype(BF)


def step_kernel(
    lengths, routes, x_hbm, og_hbm, wq, wo, wu_lin, wd_lin, vector, cls,
    out_hbm, ig_hbm, lin_q, lin_o, lin_u, lin_d, vector_out, norm_out, cls_out,
    x, dy, y, m, dh, h1, h1t, p, att, o, h2, h2t, dy16, dy16t, gdt, bias,
    wa, wu, wd, ga, gu, gd, vec, gvec, ret, heads, csend, cgot,
    slab, got, vsend, vgot, gsend, ggot,
    sb0, sb1, sb2, sb3, sb4, sb5, sb6, rb0, rb1, rb2, rb3, rb4, rb5, rb6,
    ps0, ps1, pg0, pg1, square_buf, square_got, total_buf, total_got,
    sem, send_sem, recv_sem,
    *, owners, capacity
):
    batches, rows = x.shape[0], x.shape[1]
    slots = lengths.shape[1]
    cap_pad = ret.shape[0] // owners
    is_global = lax.axis_index("dp") % 2 == 0
    length = jnp.where(is_global, LG, LF)
    layout = tiles(is_global)
    place = Place()
    d, s = place.d, place.s
    sbufs = (sb0, sb1, sb2, sb3, sb4, sb5, sb6)
    rbufs = (rb0, rb1, rb2, rb3, rb4, rb5, rb6)

    numbers = {}

    def remote(key, src, dst, device):
        n = numbers.setdefault(key, len(numbers))
        return pltpu.make_async_remote_copy(
            src_ref=src, dst_ref=dst, send_sem=send_sem.at[n], recv_sem=recv_sem.at[n],
            device_id=device, device_id_type=MESH,
        )

    sent = []

    def launch(make):
        for c in make():
            c.start()
        sent.append(make)

    def arrive(make):
        for c in make():
            c.wait_recv()

    weights = (wa, wu, wd)

    def gather_copies(g, k):
        kind, lane, width, order = GATHERS[g]
        ref = weights[kind]
        done = 0
        for e in order[:k]:
            done |= e
        found = []
        for f in subsets(order[k])[1:]:
            to = place.away(f)
            if kind < 2 and done & (X + LINE) == X + LINE:
                for c in subsets(done & 3):
                    _, bs = place.away(c)
                    at = ref.at[:, pl.ds(pl.multiple_of(bs * D + lane, 128), width)]
                    found.append(remote(("g", g, k, f, c), at, at, to))
                continue
            for c in subsets(done):
                at = ref.at[block_at(kind, place.away(c), lane, width)]
                found.append(remote(("g", g, k, f, c), at, at, to))
        return found

    def gather_stage(g, k):
        if k > 0:
            arrive(functools.partial(gather_copies, g, k - 1))
        if k < 3:
            launch(functools.partial(gather_copies, g, k))

    def vector_copies(k):
        return [
            remote(("v", k, f), vsend.at[k], vgot.at[k, n], place.away(f))
            for n, f in enumerate(subsets(VECTOR_ORDER[k])[1:])
        ]

    def vector_stage(k):
        if k > 0:
            arrive(functools.partial(vector_copies, k - 1))
            total = vsend[k - 1]
            for n in range(len(subsets(VECTOR_ORDER[k - 1])) - 1):
                total = total + vgot[k - 1, n]
            if k < 3:
                vsend[k] = total
            else:
                vec[...] = total.astype(F32)
        if k < 3:
            launch(functools.partial(vector_copies, k))

    def slab_copies():
        found = []
        for k in range(1, 4):
            j = (s + k) % 4
            found.append(remote(("s", k), slab.at[j], got.at[s], (d, j)))
        return found

    mine = pl.ds(pl.multiple_of(d * 8, 8), 8)

    def cls_copies(name, src, dst):
        found = []
        for k in range(1, owners):
            to = (d + k) % owners
            at = src.at[pl.ds(pl.multiple_of(to * 8, 8), 8)]
            found.append(remote((name, k), at, dst.at[mine], (to, s)))
        return found

    grads = (ga, gu, gd)

    def spans(g, k):
        order = REDUCES[g][3]
        rest = sum(order[k + 1 :])
        first = 0
        for i in range(k):
            first += (len(subsets(order[i])) - 1) * len(subsets(sum(order[i + 1 :])))
        return first, rest, len(subsets(rest))

    def reduce_copies(g, k):
        first, _, n = spans(g, k)
        found = []
        for i, f in enumerate(subsets(REDUCES[g][3][k])[1:]):
            at = pl.ds(first + i * n, n)
            found.append(
                remote(("r", g, k, f), sbufs[g].at[at], rbufs[g].at[at], place.away(f))
            )
        return found

    def reduce_stage(g, k):
        kind, lane, width, order = REDUCES[g]
        ref = grads[kind]
        if k > 0:
            arrive(functools.partial(reduce_copies, g, k - 1))

        def total(c):
            at = block_at(kind, place.away(c), lane, width)
            v = ref[at]
            if k > 0:
                first, rest, n = spans(g, k - 1)
                at_c = subsets(rest).index(c)
                for i in range(len(subsets(order[k - 1])) - 1):
                    v = v + rbufs[g][first + i * n + at_c].astype(F32)
            return at, v

        if k == 3:
            return total(0)[1]
        first, rest, n = spans(g, k)
        for i, f in enumerate(subsets(order[k])[1:]):
            for q, c in enumerate(subsets(rest)):
                sbufs[g][first + i * n + q] = total(f + c)[1].astype(BF)
        launch(functools.partial(reduce_copies, g, k))
        if k > 0:
            for c in subsets(rest):
                at, v = total(c)
                ref[at] = v

    def part_copies(slot):
        src, dst = (ps0, pg0) if slot == 0 else (ps1.at[slot - 1], pg1.at[slot - 1])
        found = []
        for k in range(1, 4):
            j = (s + k) % 4
            found.append(remote(("p", slot, k), src.at[j], dst.at[s], (d, j)))
        return found

    def part_start(slot, full):
        src, dst = (ps0, pg0) if slot == 0 else (ps1.at[slot - 1], pg1.at[slot - 1])
        for j in range(4):
            src[j, 0:PART] = full[j * PART : (j + 1) * PART]
        launch(functools.partial(part_copies, slot))
        dst[s] = src[s]

    def part_end(slot):
        arrive(functools.partial(part_copies, slot))
        for j in range(4):
            if slot == 0:
                for t in range(3):
                    lin_u[pl.ds(3 * j + t, PART, stride=12), :] = pg0[
                        j, 0:PART, t * 128 : (t + 1) * 128
                    ]
            elif j < 3:
                lin_q[pl.ds(3 * j + slot - 1, PART, stride=9), :] = pg1[slot - 1, j, 0:PART]
            else:
                lin_o[pl.ds(slot - 1, PART, stride=3), :] = pg1[slot - 1, j, 0:PART]

    def up_end():
        full = jnp.concatenate([reduce_stage(0, 3), reduce_stage(1, 3)], axis=1)
        part_start(0, full)

    def down_end():
        full = jnp.concatenate([reduce_stage(2, 3), reduce_stage(3, 3)], axis=1)
        for t in range(3):
            lin_d[pl.ds(t, BLOCK, stride=3), :] = full[:, t * 128 : (t + 1) * 128]

    def sums_copies(k):
        return [
            remote(("w", k, f), gsend.at[k], ggot.at[k, n], place.away(f))
            for n, f in enumerate(subsets(VECTOR_ORDER[k])[1:])
        ]

    def sums_stage(k):
        if k == 0:
            gsend[0] = gvec[...]
        else:
            arrive(functools.partial(sums_copies, k - 1))
            total = gsend[k - 1]
            for n in range(len(subsets(VECTOR_ORDER[k - 1])) - 1):
                total = total + ggot[k - 1, n]
            if k == 3:
                return total
            gsend[k] = total
        launch(functools.partial(sums_copies, k))

    copies = [
        pltpu.make_async_copy(x_hbm.at[0, b], x.at[b], sem.at[b]) for b in range(batches)
    ] + [
        pltpu.make_async_copy(og_hbm.at[0, b], dy.at[b], sem.at[batches + b])
        for b in range(batches)
    ]
    for c in copies:
        c.start()

    for j in range(4):
        for t in range(3):
            c = 3 * j + t
            lanes = slice(t * 128, (t + 1) * 128)
            if j < 3:
                part = wq[pl.ds(c, PART, stride=9), :]
            else:
                part = wo[pl.ds(t, PART, stride=3), :]
            slab[j, 0, 0:PART, lanes] = part.astype(BF)
            slab[j, 1, 0:PART, lanes] = wu_lin[pl.ds(c, PART, stride=12), :].astype(BF)
    down_rows, _ = block_at(2, (d, s), 0, D)
    for t in range(3):
        wd[down_rows, t * 128 : (t + 1) * 128] = wd_lin[pl.ds(t, BLOCK, stride=3), :].astype(BF)
    csend[...] = dg(slot_map((csend.shape[0], cls.shape[0]), 0, capacity), cls[...].astype(BF), NN)
    vrows, vcols = vector_masks(place)
    vsend[0] = dg(jnp.where(vrows, vector[...], 0.0).astype(BF), vcols.astype(BF), NN).astype(BF)

    barrier = pltpu.get_barrier_semaphore()
    peers = [(d, (s + k) % 4) for k in range(1, 4)]
    peers += [((d + k) % owners, s) for k in range(1, owners)]
    peers.append(place.away(PLANE))
    for to in peers:
        pl.semaphore_signal(barrier, inc=1, device_id=to, device_id_type=MESH)
    pl.semaphore_wait(barrier, len(peers))

    launch(slab_copies)
    vector_stage(0)
    launch(functools.partial(cls_copies, "c", csend, ret))
    got[s] = slab[s]
    ret[mine, :] = csend[mine, :]

    def segment_of(t):
        return jnp.where(
            is_global,
            (t >= LG).astype(jnp.int32) + (t >= 2 * LG).astype(jnp.int32),
            lax.shift_right_logical(t * 1772, 16),
        )

    for i, (q0, k0, lo, hi) in enumerate(layout):
        keys = segment_of(iota((WIN, TILE), 0) + k0)
        queries = segment_of(iota((WIN, TILE), 1) + q0)
        mask = jnp.where(keys == queries, 0.0, MASK_VALUE).astype(F32)
        bias[i, :, :TILE] = mask
        bias[i, :, TILE:] = mask

    arrive(slab_copies)
    for kind, ref in enumerate((wa, wu)):
        full = jnp.concatenate([got[j, kind].astype(F32)[0:PART] for j in range(4)], axis=0)
        ref[block_at(kind, (d, s), 0, D)] = full.astype(BF)
    gather_stage(0, 0)
    gather_stage(1, 0)

    def v(row):
        return vec[row : row + 1, :]

    low_half = iota((TILE, TILE), 1) < HD

    def stack(t):
        z = jnp.zeros_like(t)
        return jnp.concatenate([jnp.where(low_half, t, z), jnp.where(low_half, z, t)], axis=0)

    def unstack(t):
        return jnp.where(low_half, t[:TILE], t[TILE:])

    def rows_at(b):
        return pl.ds(pl.multiple_of(b * rows, rows), rows)

    def hook(b, at, fn):
        @pl.when(b == at)
        def _():
            fn()

    gvec[...] = jnp.zeros_like(gvec)
    for c in copies[:batches]:
        c.wait()

    def normed(b, c):
        m[b] = norm_stats(x[b])[0]
        return c

    lax.fori_loop(0, batches, normed, 0)
    vector_stage(1)
    gather_stage(0, 1)
    gather_stage(1, 1)

    def live_of(b):
        n = lengths[b, 0]
        for k in range(1, slots):
            n = n + lengths[b, k]
        return n

    def places(b, r):
        spot = jnp.full(r.shape, -1, jnp.int32)
        for k in range(slots):
            route = routes[b, k]
            padded = (route // capacity) * cap_pad + route % capacity
            padded = jnp.where(route >= 0, padded, -1)
            spot = jnp.where(r == padded, k * length, spot)
        return spot

    for c in copies[batches:]:
        c.wait()
    arrive(functools.partial(cls_copies, "c", csend, ret))

    def cotangent(b, c):
        rs = rows_at(b)
        nr = ret.shape[0]
        pick = (iota((rows, nr), 0) == places(b, iota((1, nr), 1))).astype(BF)
        live = iota((rows, D), 0) < live_of(b)
        g = dy[b] + dg(pick, ret[...].astype(BF), NN)
        g = jnp.where(live, g, 0.0)
        dy[b] = g
        g16 = g.astype(BF)
        dy16[rs, :] = g16
        dy16t[:, rs] = g16.T
        gvec[7:8, :] += jnp.sum(g16.astype(F32), axis=0, keepdims=True)
        return c

    lax.fori_loop(0, batches, cotangent, 0)
    vector_stage(2)
    gather_stage(0, 2)
    gather_stage(1, 2)
    for g in range(2, 6):
        gather_stage(g, 0)
    o[...] = jnp.zeros_like(o)
    vector_stage(3)
    gather_stage(0, 3)
    gather_stage(1, 3)

    def attend(b, c):
        rs = rows_at(b)
        h = (m[b] * v(0) + v(1)).astype(BF)
        h1[rs, :] = h
        h1t[:, rs] = h.T
        p[rs, 0:D] = (dg(h, wa[:, 0:D], NN) + v(2)).astype(BF)
        p[rs, D : 2 * D] = dg(h, wa[:, D : 2 * D], NN).astype(BF)
        p[rs, 2 * D : 3 * D] = (dg(h, wa[:, 2 * D : 3 * D], NN) + v(3)).astype(BF)
        for pair in range(PAIRS):
            c0 = pair * TILE
            for i, (q0, k0, lo, hi) in enumerate(layout):
                qr = pl.ds(pl.multiple_of(b * rows + q0, 16), TILE)
                kr = pl.ds(pl.multiple_of(b * rows + k0, 16), WIN)
                q = stack(p[qr, pl.ds(c0, TILE)] * BF(HD**-0.5))
                k = p[kr, pl.ds(D + c0, TILE)]
                val = p[kr, pl.ds(2 * D + c0, TILE)]
                sc = dg(k, q, NT) + bias[i]
                e = jnp.exp(sc - jnp.max(sc, axis=0, keepdims=True))
                a = (e * (1.0 / jnp.sum(e, axis=0, keepdims=True))).astype(BF)
                att[b, pair, i] = a
                r = unstack(dg(a, val, TN)).astype(BF)
                own = iota((TILE, TILE), 0) + q0
                own = (own >= lo) & (own < hi)
                old = o[qr, pl.ds(c0, TILE)]
                o[qr, pl.ds(c0, TILE)] = jnp.where(own, r, old)
        hook(b, 0, lambda: [gather_stage(g, 1) for g in range(2, 6)])
        hook(b, 2, lambda: [gather_stage(g, 2) for g in range(2, 6)])
        return c

    lax.fori_loop(0, batches, attend, 0)

    def middle(b, c):
        rs = rows_at(b)
        mid = x[b] + (dg(o[rs, :], wa[:, 3 * D :], NN) + v(4))
        m[b] = mid
        xhat, _ = norm_stats(mid)
        h = (xhat * v(5) + v(6)).astype(BF)
        h2[rs, :] = h
        h2t[:, rs] = h.T
        y[b] = jnp.zeros((rows, D), F32)
        dh[b] = jnp.zeros((rows, D), F32)
        return c

    lax.fori_loop(0, batches, middle, 0)
    for g in range(2, 6):
        gather_stage(g, 3)

    def chunk(j, c):
        cs = pl.ds(pl.multiple_of(j * D, D), D)
        gu[:, cs] = jnp.zeros((D, D), F32)
        gdt[...] = jnp.zeros_like(gdt)

        def mlp(b, c):
            rs = rows_at(b)
            u = dg(h2[rs, :], wu[:, cs], NN) + vec[pl.ds(8 + j, 1), :]
            g, slope = gelu_parts(u)
            g = g.astype(BF)
            y[b] += dg(g, wd[cs, :], NN)
            gdt[...] += dg(dy16t[:, rs], g, NN)
            du = (dg(dy16[rs, :], wd[cs, :], NT) * slope).astype(BF)
            gu[:, cs] += dg(h2t[:, rs], du, NN)
            dh[b] += dg(du, wu[:, cs], NT)
            gvec[pl.ds(8 + j, 1), :] += jnp.sum(du.astype(F32), axis=0, keepdims=True)
            return c

        lax.fori_loop(0, batches, mlp, 0)
        gd[cs, :] = gdt[...].T
        return c

    lax.fori_loop(0, CHUNKS, chunk, 0)
    for g in range(4):
        reduce_stage(g, 0)

    ga[:, 3 * D :] = jnp.zeros((D, D), F32)
    heads[...] = jnp.zeros_like(heads)

    def turn(b, c):
        rs = rows_at(b)
        mid = m[b]
        live = iota((rows, D), 0) < live_of(b)
        out = jnp.where(live, mid + (y[b] + v(7)), 0.0)
        y[b] = out
        nr = heads.shape[0]
        pick = (places(b, iota((nr, 1), 0)) == iota((nr, rows), 1)).astype(BF)
        heads[...] += dg(pick, out.astype(BF), NN)
        xhat, r = norm_stats(mid)
        d2 = dh[b]
        gvec[5:6, :] += jnp.sum(d2 * xhat, axis=0, keepdims=True)
        gvec[6:7, :] += jnp.sum(d2, axis=0, keepdims=True)
        dm = dy[b] + norm_back(d2, v(5), xhat, r)
        dy[b] = dm
        d16 = dm.astype(BF)
        gvec[4:5, :] += jnp.sum(d16.astype(F32), axis=0, keepdims=True)
        ga[:, 3 * D :] += dg(o[rs, :], d16, TN)
        h2[rs, :] = dg(d16, wa[:, 3 * D :], NT).astype(BF)
        dh[b] = jnp.zeros((rows, D), F32)
        hook(b, 2, lambda: [reduce_stage(g, 1) for g in range(4)])
        return c

    lax.fori_loop(0, batches, turn, 0)
    outs = [pltpu.make_async_copy(y.at[b], out_hbm.at[0, b], sem.at[b]) for b in range(batches)]
    for c in outs:
        c.start()
    launch(functools.partial(cls_copies, "h", heads, cgot))
    cgot[mine, :] = heads[mine, :]

    dp = dy16
    hooks = {
        (0, 3): lambda: [reduce_stage(g, 2) for g in range(4)],
        (1, 0): lambda: reduce_stage(4, 1),
        (1, 1): lambda: (up_end(), down_end()),
        (1, 2): lambda: reduce_stage(4, 2),
        (1, 3): lambda: part_end(0),
        (2, 0): lambda: (part_start(1, reduce_stage(4, 3)), reduce_stage(5, 1)),
        (2, 2): lambda: (part_end(1), reduce_stage(5, 2)),
    }
    for pair in range(PAIRS):
        c0 = pair * TILE

        def attend_back(b, c, pair=pair, c0=c0):
            rs = rows_at(b)
            y_k, y_v = m.at[0, :, 0:TILE], m.at[0, :, TILE : 2 * TILE]
            m[0, :, 0 : 2 * TILE] = jnp.zeros((rows, 2 * TILE), F32)
            for i, (q0, k0, lo, hi) in enumerate(layout):
                qr = pl.ds(pl.multiple_of(b * rows + q0, 16), TILE)
                kr = pl.ds(pl.multiple_of(b * rows + k0, 16), WIN)
                wr = pl.ds(pl.multiple_of(k0, 16), WIN)
                own = iota((TILE, TILE), 0) + q0
                own = (own >= lo) & (own < hi)
                do = h2[qr, pl.ds(c0, TILE)]
                do = stack(jnp.where(own, do, jnp.zeros_like(do)))
                q = stack(p[qr, pl.ds(c0, TILE)] * BF(HD**-0.5))
                k = p[kr, pl.ds(D + c0, TILE)]
                val = p[kr, pl.ds(2 * D + c0, TILE)]
                a = att[b, pair, i]
                af = a.astype(F32)
                da = dg(val, do, NT)
                ds = af * (da - jnp.sum(af * da, axis=0, keepdims=True))
                ds = ds.astype(BF)
                dq = (unstack(dg(ds, k, TN)) * HD**-0.5).astype(BF)
                old = dp[qr, pl.ds(0, TILE)]
                dp[qr, pl.ds(0, TILE)] = jnp.where(own, dq, old)
                y_k[wr, :] += dg(ds, q, NN)
                y_v[wr, :] += dg(a, do, NN)
            dp[rs, TILE : 2 * TILE] = y_k[...].astype(BF)
            dp[rs, 2 * TILE :] = y_v[...].astype(BF)
            w = jnp.concatenate(
                [wa[:, i * D + c0 : i * D + c0 + TILE] for i in range(3)], axis=1
            )
            dh[b] += dg(dp[rs, :], w, NT)
            for (at_pair, at_b), fn in hooks.items():
                if at_pair == pair:
                    hook(b, at_b, fn)
            return c

        dp[:, 0:TILE] = jnp.zeros((batches * rows, TILE), BF)
        lax.fori_loop(0, batches, attend_back, 0)
        g = dg(h1t[...], dp[...], NN)
        sums = jnp.sum(dp[...].astype(F32), axis=0, keepdims=True)
        gvec[2:3, c0 : c0 + TILE] = sums[:, 0:TILE]
        gvec[3:4, c0 : c0 + TILE] = sums[:, 2 * TILE :]
        for i in range(3):
            ga[:, i * D + c0 : i * D + c0 + TILE] = g[:, i * TILE : (i + 1) * TILE]
        reduce_stage(4 + pair, 0)
        if pair == 2:
            part_start(2, reduce_stage(5, 3))

    for c in outs:
        c.wait()

    def last(b, c):
        xhat, r = norm_stats(x[b])
        d1 = dh[b]
        gvec[0:1, :] += jnp.sum(d1 * xhat, axis=0, keepdims=True)
        gvec[1:2, :] += jnp.sum(d1, axis=0, keepdims=True)
        y[b] = dy[b] + norm_back(d1, v(0), xhat, r)
        hook(b, 0, lambda: reduce_stage(6, 1))
        return c

    lax.fori_loop(0, batches, last, 0)
    outs = [pltpu.make_async_copy(y.at[b], ig_hbm.at[0, b], sem.at[b]) for b in range(batches)]
    for c in outs:
        c.start()
    sums_stage(0)
    part_end(2)
    reduce_stage(6, 2)
    arrive(functools.partial(cls_copies, "h", heads, cgot))
    pick = slot_map((cls_out.shape[0], cgot.shape[0]), 1, capacity)
    cls_out[...] = dg(pick, cgot[...].astype(BF), NN)
    sums_stage(1)
    part_start(3, reduce_stage(6, 3))
    sums_stage(2)
    part_end(3)
    sums = sums_stage(3)
    vrows, vcols = vector_masks(place)
    own_sums = lax.dot_general(
        sums, vcols.astype(F32), NT, precision=lax.Precision.HIGHEST, preferred_element_type=F32
    )
    own_sums = jnp.sum(jnp.where(vrows, own_sums, 0.0), axis=0, keepdims=True)
    vector_out[...] = own_sums

    squares = jnp.zeros((1, 128), F32)
    for ref in (lin_q, lin_o, lin_u, lin_d):
        g = ref[...]
        squares = squares + jnp.sum(g * g, axis=0, keepdims=True)
    squares = jnp.sum(squares, axis=1, keepdims=True)
    squares = squares + jnp.sum(own_sums * own_sums, axis=1, keepdims=True)
    square_buf[...] = jnp.broadcast_to(squares, (8, 128))

    def square_copies():
        return [
            remote(("q", k), square_buf, square_got.at[s], (d, (s + k) % 4)) for k in range(1, 4)
        ]

    def total_copies():
        return [
            remote(("t", k), total_buf, total_got.at[d], ((d + k) % owners, s))
            for k in range(1, owners)
        ]

    launch(square_copies)
    square_got[s] = square_buf[...]
    arrive(square_copies)
    total_buf[...] = (square_got[0] + square_got[1]) + (square_got[2] + square_got[3])
    launch(total_copies)
    total_got[d] = total_buf[...]
    arrive(total_copies)
    total = total_got[0]
    for k in range(1, owners):
        total = total + total_got[k]
    norm_out[...] = jnp.sqrt(total)
    for c in outs:
        c.wait()
    for make in sent:
        for c in make():
            c.wait_send()


def run_step(lengths, routes, x, og, masters, cls, owners, capacity):
    qkv, out, up, down, vector = masters
    lin = [w.reshape(-1, 128) for w in (qkv, out, up, down)]
    batches, rows = x.shape[1], x.shape[2]
    total = batches * rows
    slots = owners * 8
    vm = pl.BlockSpec(memory_space=VM)
    sm = pl.BlockSpec(memory_space=pltpu.SMEM)
    anyspace = pl.BlockSpec(memory_space=pl.ANY)
    act = VM((total, D), BF)
    actt = VM((D, total), BF)
    full = VM((batches, rows, D), F32)
    scratch = [
        full, full, full, full, full,
        act, actt, VM((total, 3 * D), BF), VM((batches, PAIRS, 4, WIN, 2 * TILE), BF),
        act, act, actt, act, actt, VM((D, D), F32), VM((4, WIN, 2 * TILE), F32),
        VM((D, 4 * D), BF), VM((D, FF), BF), VM((FF, D), BF),
        VM((D, 4 * D), F32), VM((D, FF), F32), VM((FF, D), F32),
        VM((16, D), F32), VM((16, D), F32),
        VM((slots, D), F32), VM((slots, D), F32), VM((slots, D), F32), VM((slots, D), F32),
        VM((4, 2, 16, D), BF), VM((4, 2, 16, D), BF),
        VM((3, 16, D), BF), VM((3, 3, 16, D), BF), VM((3, 16, D), F32), VM((3, 3, 16, D), F32),
    ]
    buffers = [VM((31, BLOCK, r[2]), BF) for r in REDUCES]
    scratch += buffers + buffers
    scratch += [
        VM((4, 16, D), F32), VM((3, 4, 16, 128), F32),
        VM((4, 16, D), F32), VM((3, 4, 16, 128), F32),
        VM((8, 128), F32), VM((4, 8, 128), F32), VM((8, 128), F32), VM((owners, 8, 128), F32),
        pltpu.SemaphoreType.DMA((2 * batches,)),
        pltpu.SemaphoreType.DMA((256,)), pltpu.SemaphoreType.DMA((256,)),
    ]
    return pl.pallas_call(
        functools.partial(step_kernel, owners=owners, capacity=capacity),
        out_shape=(
            jax.ShapeDtypeStruct(x.shape, F32), jax.ShapeDtypeStruct(x.shape, F32),
        ) + tuple(jax.ShapeDtypeStruct(w.shape, F32) for w in lin) + (
            jax.ShapeDtypeStruct((1, vector.shape[0]), F32),
            jax.ShapeDtypeStruct((8, 128), F32),
            jax.ShapeDtypeStruct((owners * capacity, D), F32),
        ),
        in_specs=[sm, sm, anyspace, anyspace] + [vm] * 6,
        out_specs=(anyspace, anyspace) + (vm,) * 7,
        scratch_shapes=scratch,
        compiler_params=pltpu.CompilerParams(
            collective_id=1, has_side_effects=True, vmem_limit_bytes=63 * 2**20
        ),
        name="step",
    )(lengths, routes, x, og, *lin, vector.reshape(1, -1), cls)


def adam_terms(master, first, second, gradient, factor, rate, decay):
    clipped = gradient * factor
    mean = BETA_ONE * first + (1.0 - BETA_ONE) * clipped
    square = BETA_TWO * second + (1.0 - BETA_TWO) * clipped * clipped
    mean_hat = mean / (1.0 - BETA_ONE**STEP_NUM)
    square_hat = square / (1.0 - BETA_TWO**STEP_NUM)
    step = mean_hat / (jnp.sqrt(square_hat) + ADAM_EPSILON)
    return master - rate * (step + decay * master), mean, square


def update_kernel(*refs):
    block_in, grad_in, norm, cls_in = refs[:4]
    grads, state = refs[4:9], refs[9:24]
    block_out, grad_out, cls_out, norm_out = refs[24:28]
    results, sem = refs[28:43], refs[43]
    batches = block_in.shape[1]
    copies = []
    for i, (src, dst) in enumerate(((block_in, block_out), (grad_in, grad_out))):
        for b in range(batches):
            c = pltpu.make_async_copy(src.at[0, b], dst.at[0, b], sem.at[i * batches + b])
            c.start()
            copies.append(c)
    cls_out[...] = cls_in[...]
    value = norm[0:1, 0:1]
    norm_out[...] = value
    factor = jnp.minimum(1.0, CLIP_LIMIT / value)
    for i in range(5):
        rate, decay = (RATE_VECTOR, 0.0) if i == 4 else (RATE_MATRIX, WEIGHT_DECAY)
        new = adam_terms(
            state[i][...], state[5 + i][...], state[10 + i][...], grads[i][...],
            factor, rate, decay,
        )
        for k in range(3):
            results[5 * k + i][...] = new[k]
    for c in copies:
        c.wait()


def run_update(block_out, input_grad, norm, cls_grouped, grads, state):
    flat = [w.reshape(1, -1) if i % 5 == 4 else w.reshape(-1, 128) for i, w in enumerate(state)]
    vm = pl.BlockSpec(memory_space=VM)
    anyspace = pl.BlockSpec(memory_space=pl.ANY)
    shapes = [block_out.shape, input_grad.shape, cls_grouped.shape, (1, 1)]
    shapes += [w.shape for w in flat]
    return pl.pallas_call(
        update_kernel,
        out_shape=tuple(jax.ShapeDtypeStruct(z, F32) for z in shapes),
        in_specs=[anyspace, anyspace] + [vm] * 22,
        out_specs=(anyspace, anyspace) + (vm,) * 17,
        scratch_shapes=[pltpu.SemaphoreType.DMA((2 * block_out.shape[1],))],
        compiler_params=pltpu.CompilerParams(vmem_limit_bytes=16 * 2**20),
        name="update",
    )(block_out, input_grad, norm, cls_grouped, *grads, *flat)


def local_fast(tokens, out_grad, cls_grad, crop_lengths, cls_route, *state):
    owners = lax.axis_size("dp")
    capacity = cls_grad.shape[0] // owners
    done = run_step(
        crop_lengths[0], cls_route[0], tokens, out_grad, state[:5], cls_grad, owners, capacity
    )
    block_out, input_grad = done[:2]
    new = run_update(block_out, input_grad, done[7], done[8], done[2:7], state)
    rest = tuple(w.reshape(-1) for w in new[4:])
    return (new[0], new[2], new[1], new[3].reshape(())) + rest


def solution(mesh):
    spread = ("dp", "shard")
    in_specs = (
        P(spread, None, None, None), P(spread, None, None, None), P(spread, None),
        P(spread, None, None), P(spread, None, None),
    ) + (P(spread),) * 15
    out_specs = (
        P(spread, None, None, None), P(spread, None), P(spread, None, None, None), P(),
    ) + (P(spread),) * 15
    fast = mesh.shape["shard"] == 4 and mesh.shape["dp"] == 8
    body = local_fast if fast else local
    return jax.shard_map(body, mesh=mesh, in_specs=in_specs, out_specs=out_specs, check_vma=False)
```

```python
import functools

import jax
import jax.numpy as jnp
from jax import lax
from jax.experimental import pallas as pl
from jax.experimental.pallas import tpu as pltpu
from jax.sharding import PartitionSpec as P

D = 384
H = 6
HD = 64
FF = 1536
STEP_NUM = 10
LG = 197
LF = 37

NORM_EPSILON = 1e-06
BETA_ONE = 0.9
BETA_TWO = 0.999
ADAM_EPSILON = 1e-08
RATE_MATRIX = 0.05
RATE_VECTOR = 0.3
WEIGHT_DECAY = 0.05
CLIP_LIMIT = 1.0
MASK_VALUE = -1e30

BF = jnp.bfloat16
F32 = jnp.float32
NN = (((1,), (0,)), ((), ()))
NT = (((1,), (1,)), ((), ()))
TN = (((0,), (0,)), ((), ()))
PAIRS = H // 2
CHUNKS = FF // D
TILE = 128
WIN = 256


def dg(a, b, dims):
    return lax.dot_general(a, b, dims, preferred_element_type=F32)


def iota(shape, dim):
    return lax.broadcasted_iota(jnp.int32, shape, dim)


def tiles(is_global):
    focal = ((0, 0, 0, 128), (128, 64, 128, 256), (256, 192, 256, 384), (384, 256, 384, 512))
    whole = ((0, 0, 0, 128), (80, 0, 128, 197), (192, 192, 197, 320), (272, 192, 320, 394))
    return [
        tuple(jnp.where(is_global, w, f) for w, f in zip(whole[i], focal[i])) for i in range(4)
    ]


def norm_stats(v):
    mean = jnp.mean(v, axis=-1, keepdims=True)
    c = v - mean
    var = jnp.mean(c * c, axis=-1, keepdims=True)
    r = lax.rsqrt(var + NORM_EPSILON)
    return c * r, r


def norm_back(dh, gain, xhat, r):
    d = dh * gain
    m1 = jnp.mean(d, axis=-1, keepdims=True)
    m2 = jnp.mean(d * xhat, axis=-1, keepdims=True)
    return (d - m1 - xhat * m2) * r


def gelu_parts(u):
    cdf = 0.5 + 0.5 * lax.erf(u * 0.7071067811865476)
    pdf = jnp.exp(u * u * -0.5) * 0.3989422804014327
    return u * cdf, cdf + u * pdf


def main_kernel(
    lengths, routes, x_hbm, og_hbm, wa, wu, wd, vec, ret,
    out_hbm, ig_hbm, ga, gu, gd, gvec, heads,
    x, dy, y, m, dh, h1, h1t, p, att, o, h2, h2t, dy16, dy16t, dp, gdt, bias, sem,
    *, capacity, owners, stages
):
    batches, rows = x.shape[0], x.shape[1]
    slots = lengths.shape[1]
    cap_pad = ret.shape[0] // owners
    is_global = lax.axis_index("dp") % 2 == 0
    length = jnp.where(is_global, LG, LF)
    layout = tiles(is_global)

    copies = [
        pltpu.make_async_copy(x_hbm.at[0, b], x.at[b], sem.at[b]) for b in range(batches)
    ] + [
        pltpu.make_async_copy(og_hbm.at[0, b], dy.at[b], sem.at[batches + b])
        for b in range(batches)
    ]
    for c in copies:
        c.start()

    def segment_of(t):
        return jnp.where(
            is_global,
            (t >= LG).astype(jnp.int32) + (t >= 2 * LG).astype(jnp.int32),
            lax.shift_right_logical(t * 1772, 16),
        )

    for i, (q0, k0, lo, hi) in enumerate(layout):
        keys = segment_of(iota((WIN, TILE), 0) + k0)
        queries = segment_of(iota((WIN, TILE), 1) + q0)
        mask = jnp.where(keys == queries, 0.0, MASK_VALUE).astype(F32)
        bias[i, :, :TILE] = mask
        bias[i, :, TILE:] = mask

    def v(row):
        return vec[row : row + 1, :]

    low_half = iota((TILE, TILE), 1) < HD

    def stack(t):
        z = jnp.zeros_like(t)
        return jnp.concatenate([jnp.where(low_half, t, z), jnp.where(low_half, z, t)], axis=0)

    def unstack(t):
        return jnp.where(low_half, t[:TILE], t[TILE:])

    def rows_at(b):
        return pl.ds(pl.multiple_of(b * rows, rows), rows)

    gvec[...] = jnp.zeros_like(gvec)
    if "f1" in stages:
        for b in range(batches):
            copies[b].wait()

        def attend(b, c):
            rs = rows_at(b)
            xhat, _ = norm_stats(x[b])
            h = (xhat * v(0) + v(1)).astype(BF)
            h1[rs, :] = h
            h1t[:, rs] = h.T
            p[rs, 0:D] = (dg(h, wa[:, 0:D], NN) + v(2)).astype(BF)
            p[rs, D : 2 * D] = dg(h, wa[:, D : 2 * D], NN).astype(BF)
            p[rs, 2 * D : 3 * D] = (dg(h, wa[:, 2 * D : 3 * D], NN) + v(3)).astype(BF)
            for pair in range(PAIRS if "at" in stages else 0):
                c0 = pair * TILE
                for i, (q0, k0, lo, hi) in enumerate(layout):
                    qr = pl.ds(pl.multiple_of(b * rows + q0, 16), TILE)
                    kr = pl.ds(pl.multiple_of(b * rows + k0, 16), WIN)
                    q = stack(p[qr, pl.ds(c0, TILE)] * BF(HD**-0.5))
                    k = p[kr, pl.ds(D + c0, TILE)]
                    val = p[kr, pl.ds(2 * D + c0, TILE)]
                    s = dg(k, q, NT) + bias[i]
                    e = jnp.exp(s - jnp.max(s, axis=0, keepdims=True))
                    a = (e * (1.0 / jnp.sum(e, axis=0, keepdims=True))).astype(BF)
                    att[b, pair, i] = a
                    r = unstack(dg(a, val, TN)).astype(BF)
                    own = iota((TILE, TILE), 0) + q0
                    own = (own >= lo) & (own < hi)
                    old = o[qr, pl.ds(c0, TILE)]
                    o[qr, pl.ds(c0, TILE)] = jnp.where(own, r, old)
            return c

        o[...] = jnp.zeros_like(o)
        lax.fori_loop(0, batches, attend, 0)

    def live_of(b):
        n = lengths[b, 0]
        for k in range(1, slots):
            n = n + lengths[b, k]
        return n

    def places(b, r):
        spot = jnp.full(r.shape, -1, jnp.int32)
        for k in range(slots):
            route = routes[b, k]
            padded = (route // capacity) * cap_pad + route % capacity
            padded = jnp.where(route >= 0, padded, -1)
            spot = jnp.where(r == padded, k * length, spot)
        return spot

    if "f1b" in stages:
        for b in range(batches):
            copies[batches + b].wait()

        def middle(b, c):
            rs = rows_at(b)
            mid = x[b] + (dg(o[rs, :], wa[:, 3 * D :], NN) + v(4))
            m[b] = mid
            xhat, _ = norm_stats(mid)
            h = (xhat * v(5) + v(6)).astype(BF)
            h2[rs, :] = h
            h2t[:, rs] = h.T
            nr = ret.shape[0]
            pick = (iota((rows, nr), 0) == places(b, iota((1, nr), 1))).astype(BF)
            live = iota((rows, D), 0) < live_of(b)
            g = dy[b] + dg(pick, ret[...].astype(BF), NN)
            g = jnp.where(live, g, 0.0)
            dy[b] = g
            g16 = g.astype(BF)
            dy16[rs, :] = g16
            dy16t[:, rs] = g16.T
            gvec[7:8, :] += jnp.sum(g16.astype(F32), axis=0, keepdims=True)
            y[b] = jnp.zeros((rows, D), F32)
            dh[b] = jnp.zeros((rows, D), F32)
            return c

        lax.fori_loop(0, batches, middle, 0)

    if "f2" in stages:
        gu[...] = jnp.zeros_like(gu)
        gdt[...] = jnp.zeros_like(gdt)

        def mlp(t, c):
            j, b = t // batches, t % batches
            rs = rows_at(b)
            cs = pl.ds(pl.multiple_of(j * D, D), D)
            u = dg(h2[rs, :], wu[:, cs], NN) + vec[pl.ds(8 + j, 1), :]
            g, slope = gelu_parts(u)
            g = g.astype(BF)
            y[b] += dg(g, wd[cs, :], NN)
            gdt[:, cs] += dg(dy16t[:, rs], g, NN)
            du = (dg(dy16[rs, :], wd[cs, :], NT) * slope).astype(BF)
            gu[:, cs] += dg(h2t[:, rs], du, NN)
            dh[b] += dg(du, wu[:, cs], NT)
            gvec[pl.ds(8 + j, 1), :] += jnp.sum(du.astype(F32), axis=0, keepdims=True)
            return c

        lax.fori_loop(0, CHUNKS * batches, mlp, 0)
        for j in range(CHUNKS):
            gd[j * D : (j + 1) * D, :] = gdt[:, j * D : (j + 1) * D].T

    if "f2b" in stages:
        ga[:, 3 * D :] = jnp.zeros((D, D), F32)
        heads[...] = jnp.zeros_like(heads)

        def turn(b, c):
            rs = rows_at(b)
            mid = m[b]
            live = iota((rows, D), 0) < live_of(b)
            out = jnp.where(live, mid + (y[b] + v(7)), 0.0)
            y[b] = out
            nr = heads.shape[0]
            pick = (places(b, iota((nr, 1), 0)) == iota((nr, rows), 1)).astype(BF)
            heads[...] += dg(pick, out.astype(BF), NN)
            xhat, r = norm_stats(mid)
            d2 = dh[b]
            gvec[5:6, :] += jnp.sum(d2 * xhat, axis=0, keepdims=True)
            gvec[6:7, :] += jnp.sum(d2, axis=0, keepdims=True)
            dm = dy[b] + norm_back(d2, v(5), xhat, r)
            dy[b] = dm
            d16 = dm.astype(BF)
            gvec[4:5, :] += jnp.sum(d16.astype(F32), axis=0, keepdims=True)
            ga[:, 3 * D :] += dg(o[rs, :], d16, TN)
            h2[rs, :] = dg(d16, wa[:, 3 * D :], NT).astype(BF)
            dh[b] = jnp.zeros((rows, D), F32)
            return c

        lax.fori_loop(0, batches, turn, 0)
        outs = [
            pltpu.make_async_copy(y.at[b], out_hbm.at[0, b], sem.at[b]) for b in range(batches)
        ]
        for c in outs:
            c.start()

    if "b1" in stages:
        for pair in range(PAIRS):
            c0 = pair * TILE

            def attend_back(b, c):
                rs = rows_at(b)
                y_k, y_v = m.at[0, :, 0:TILE], m.at[0, :, TILE : 2 * TILE]
                m[0, :, 0 : 2 * TILE] = jnp.zeros((rows, 2 * TILE), F32)
                for i, (q0, k0, lo, hi) in enumerate(layout):
                    qr = pl.ds(pl.multiple_of(b * rows + q0, 16), TILE)
                    kr = pl.ds(pl.multiple_of(b * rows + k0, 16), WIN)
                    wr = pl.ds(pl.multiple_of(k0, 16), WIN)
                    own = iota((TILE, TILE), 0) + q0
                    own = (own >= lo) & (own < hi)
                    do = h2[qr, pl.ds(c0, TILE)]
                    do = stack(jnp.where(own, do, jnp.zeros_like(do)))
                    q = stack(p[qr, pl.ds(c0, TILE)] * BF(HD**-0.5))
                    k = p[kr, pl.ds(D + c0, TILE)]
                    val = p[kr, pl.ds(2 * D + c0, TILE)]
                    a = att[b, pair, i]
                    af = a.astype(F32)
                    da = dg(val, do, NT)
                    ds = af * (da - jnp.sum(af * da, axis=0, keepdims=True))
                    ds = ds.astype(BF)
                    dq = (unstack(dg(ds, k, TN)) * HD**-0.5).astype(BF)
                    old = dp[qr, pl.ds(0, TILE)]
                    dp[qr, pl.ds(0, TILE)] = jnp.where(own, dq, old)
                    y_k[wr, :] += dg(ds, q, NN)
                    y_v[wr, :] += dg(a, do, NN)
                dp[rs, TILE : 2 * TILE] = y_k[...].astype(BF)
                dp[rs, 2 * TILE :] = y_v[...].astype(BF)
                w = jnp.concatenate(
                    [wa[:, s * D + c0 : s * D + c0 + TILE] for s in range(3)], axis=1
                )
                dh[b] += dg(dp[rs, :], w, NT)
                return c

            dp[:, 0:TILE] = jnp.zeros((batches * rows, TILE), BF)
            lax.fori_loop(0, batches, attend_back, 0)
            g = dg(h1t[...], dp[...], NN)
            sums = jnp.sum(dp[...].astype(F32), axis=0, keepdims=True)
            gvec[2:3, c0 : c0 + TILE] = sums[:, 0:TILE]
            gvec[3:4, c0 : c0 + TILE] = sums[:, 2 * TILE :]
            for s in range(3):
                ga[:, s * D + c0 : s * D + c0 + TILE] = g[:, s * TILE : (s + 1) * TILE]

    if "b2" in stages:
        for c in outs:
            c.wait()

        def last(b, c):
            xhat, r = norm_stats(x[b])
            d1 = dh[b]
            gvec[0:1, :] += jnp.sum(d1 * xhat, axis=0, keepdims=True)
            gvec[1:2, :] += jnp.sum(d1, axis=0, keepdims=True)
            y[b] = dy[b] + norm_back(d1, v(0), xhat, r)
            return c

        lax.fori_loop(0, batches, last, 0)
        outs = [
            pltpu.make_async_copy(y.at[b], ig_hbm.at[0, b], sem.at[b]) for b in range(batches)
        ]
        for c in outs:
            c.start()
        for c in outs:
            c.wait()


STAGES = ("f1", "at", "f1b", "f2", "f2b", "b1", "b2")


def run_main(lengths, routes, x, og, wa, wu, wd, vec, ret, capacity, owners, stages=STAGES):
    batches, rows = x.shape[1], x.shape[2]
    total = batches * rows
    vm = pl.BlockSpec(memory_space=pltpu.VMEM)
    sm = pl.BlockSpec(memory_space=pltpu.SMEM)
    anyspace = pl.BlockSpec(memory_space=pl.ANY)
    out_shape = (
        jax.ShapeDtypeStruct(x.shape, F32),
        jax.ShapeDtypeStruct(x.shape, F32),
        jax.ShapeDtypeStruct((D, 4 * D), F32),
        jax.ShapeDtypeStruct((D, FF), F32),
        jax.ShapeDtypeStruct((FF, D), F32),
        jax.ShapeDtypeStruct((16, D), F32),
        jax.ShapeDtypeStruct(ret.shape, F32),
    )
    act = pltpu.VMEM((total, D), BF)
    actt = pltpu.VMEM((D, total), BF)
    full = pltpu.VMEM((batches, rows, D), F32)
    scratch = [
        full, full, full, full, full,
        act, actt, pltpu.VMEM((total, 3 * D), BF),
        pltpu.VMEM((batches, PAIRS, 4, WIN, 2 * TILE), BF),
        act, act, actt, act, actt, act,
        pltpu.VMEM((D, FF), F32),
        pltpu.VMEM((4, WIN, 2 * TILE), F32),
        pltpu.SemaphoreType.DMA((2 * batches,)),
    ]
    return pl.pallas_call(
        functools.partial(main_kernel, capacity=capacity, owners=owners, stages=stages),
        out_shape=out_shape,
        in_specs=[sm, sm, anyspace, anyspace, vm, vm, vm, vm, vm],
        out_specs=(anyspace, anyspace, vm, vm, vm, vm, vm),
        scratch_shapes=scratch,
        compiler_params=pltpu.CompilerParams(vmem_limit_bytes=62 * 2**20),
        name="step_main",
    )(lengths, routes, x, og, wa, wu, wd, vec, ret)


def adam_update(master, moment_one, second, gradient, factor, step_rate, decay_rate):
    clipped = gradient * factor
    mean_new = BETA_ONE * moment_one + (1.0 - BETA_ONE) * clipped
    square_new = BETA_TWO * second + (1.0 - BETA_TWO) * clipped * clipped
    mean_hat = mean_new / (1.0 - BETA_ONE**STEP_NUM)
    square_hat = square_new / (1.0 - BETA_TWO**STEP_NUM)
    updated = master - step_rate * (
        mean_hat / (jnp.sqrt(square_hat) + ADAM_EPSILON) + decay_rate * master
    )
    return (updated, mean_new, square_new)


def pad_slots(a, owners, capacity, cap_pad):
    a = a.reshape(owners, capacity, D)
    return jnp.pad(a, ((0, 0), (0, cap_pad - capacity), (0, 0))).reshape(owners * cap_pad, D)


def local(tokens, out_grad, cls_grad, crop_lengths, cls_route, *state):
    masters, firsts, seconds = state[:5], state[5:10], state[10:15]
    axes = ("dp", "shard")
    owners = lax.axis_size("dp")
    capacity = cls_grad.shape[0] // owners
    cap_pad = -(-capacity // 8) * 8
    qkv, out, up, down, vector = (
        lax.all_gather(w.astype(BF), axes, axis=0, tiled=True) for w in masters
    )
    wa = jnp.concatenate([qkv.reshape(D, 3 * D), out.reshape(D, D)], axis=1)
    vec = jnp.pad(vector.astype(F32).reshape(12, D), ((0, 4), (0, 0)))
    returned = lax.all_to_all(
        cls_grad.reshape(owners, capacity, D).astype(BF), "dp", 0, 0, tiled=True
    )
    ret = pad_slots(returned.astype(F32), owners, capacity, cap_pad)
    block_out, input_grad, ga, gu, gd, gvec, heads = run_main(
        crop_lengths[0], cls_route[0], tokens, out_grad,
        wa, up.reshape(D, FF), down.reshape(FF, D), vec, ret, capacity, owners,
    )
    heads = heads.reshape(owners, cap_pad, D)[:, :capacity].astype(BF)
    cls_grouped = lax.all_to_all(heads, "dp", 0, 0, tiled=True).astype(F32)
    cls_grouped = cls_grouped.reshape(owners * capacity, D)
    grads = (ga[:, : 3 * D], ga[:, 3 * D :], gu, gd, gvec[:12])
    grads = [
        lax.psum_scatter(g.reshape(-1), axes, scatter_dimension=0, tiled=True) for g in grads
    ]
    grad_norm = jnp.sqrt(lax.psum(sum(jnp.sum(g * g) for g in grads), axes))
    factor = jnp.minimum(1.0, CLIP_LIMIT / grad_norm)
    rates = (RATE_MATRIX,) * 4 + (RATE_VECTOR,)
    decays = (WEIGHT_DECAY,) * 4 + (0.0,)
    new = [
        adam_update(masters[i], firsts[i], seconds[i], grads[i], factor, rates[i], decays[i])
        for i in range(5)
    ]
    return (block_out, cls_grouped, input_grad, grad_norm) + tuple(
        new[i][k] for k in range(3) for i in range(5)
    )


MESH = pl.DeviceIdType.MESH
VM = pltpu.VMEM
CORE, Y, X, Z_LOW, Z_HIGH = 1, 2, 4, 8, 16
PLANE, LINE = X + Y, Z_LOW + Z_HIGH
BLOCK = 48
PART = 12
GATHERS = (
    (0, 0, 256, (LINE, PLANE, CORE)),
    (0, 256, 128, (PLANE, LINE, CORE)),
    (1, 0, 256, (LINE, PLANE, CORE)),
    (1, 256, 128, (PLANE, LINE, CORE)),
    (2, 0, 256, (LINE, PLANE, CORE)),
    (2, 256, 128, (PLANE, LINE, CORE)),
)
REDUCES = (
    (1, 0, 256, (CORE, PLANE, LINE)),
    (1, 256, 128, (CORE, LINE, PLANE)),
    (2, 0, 256, (CORE, PLANE, LINE)),
    (2, 256, 128, (CORE, LINE, PLANE)),
    (0, 0, 128, (CORE, PLANE, LINE)),
    (0, 128, 128, (CORE, PLANE, LINE)),
    (0, 256, 128, (CORE, PLANE, LINE)),
)
VECTOR_ORDER = (LINE, PLANE, CORE)
SUMS_ORDER = (CORE, PLANE, LINE)


def subsets(bits):
    found = [0]
    for b in (1, 2, 4, 8, 16):
        if bits & b:
            found = found + [c + b for c in found]
    return found


class Place:
    def __init__(self):
        self.d = lax.axis_index("dp")
        self.s = lax.axis_index("shard")

    def away(self, flips):
        d, s = self.d, self.s
        for b in (1, 2):
            if flips & b:
                s = s + b * (1 - 2 * ((self.s // b) % 2))
        for b in (4, 8, 16):
            if flips & b:
                d = d + (b // 4) * (1 - 2 * ((self.d // (b // 4)) % 2))
        return d, s


def block_at(kind, where, lane, width):
    d, s = where
    if kind < 2:
        rows = pl.ds(pl.multiple_of(d * BLOCK, 16), BLOCK)
        return rows, pl.ds(pl.multiple_of(s * D + lane, 128), width)
    return pl.ds(pl.multiple_of((d * 4 + s) * BLOCK, 16), BLOCK), pl.ds(lane, width)


def vector_masks(place):
    span = 12 * D // 32
    first = (place.d * 4 + place.s) * span
    flat = iota((16, span), 1) + first
    row = iota((16, span), 0)
    rows = (flat >= row * D) & (flat < (row + 1) * D)
    col = iota((span, D), 1)
    at = iota((span, D), 0) + first
    cols = jnp.zeros((span, D), jnp.bool_)
    for k in range(12):
        cols = cols | (at - k * D == col)
    return rows, cols


def slot_map(shape, dim, capacity):
    padded, plain = iota(shape, dim), iota(shape, 1 - dim)
    owner = lax.shift_right_logical(padded, 3)
    inner = padded - owner * 8
    return ((inner < capacity) & (owner * capacity + inner == plain)).astype(BF)


def step_kernel(
    lengths_hbm, routes_hbm, x_hbm, og_hbm, wq_hbm, wo_hbm, wu_hbm, wd_hbm, vector_hbm, cls_hbm,
    y, dy, lin, cls_out,
    wq, wo, wu_lin, wd_lin, vector, cls, lengths, routes,
    x, hat, h1, h1t, p, att, o, h2, dy16, gb, dub, gdt, bup, gbup, dqs, bias,
    wa, wu, wd, ga, gu, gd, vec, gvec, ret, heads, csend, cgot,
    slab, got, vsend, vgot, gsend, ggot,
    sb0, sb1, sb2, sb3, sb4, sb5, sb6, rb0, rb1, rb2, rb3, rb4, rb5, rb6,
    ps0, ps1, pg0, pg1, square_buf, square_got, late_buf, late_got,
    sem, send_sem, recv_sem, all_sem,
    *, owners, capacity
):
    batches, rows = x.shape[0], x.shape[1]
    slots = lengths.shape[1]
    cap_pad = ret.shape[0] // owners
    is_global = lax.axis_index("dp") % 2 == 0
    length = jnp.where(is_global, LG, LF)
    layout = tiles(is_global)
    place = Place()
    d, s = place.d, place.s
    lin_q, lin_o = lin.at[0:108], lin.at[112:148]
    lin_u, lin_d = lin.at[152:296], lin.at[296:440]
    sbufs = (sb0, sb1, sb2, sb3, sb4, sb5, sb6)
    rbufs = (rb0, rb1, rb2, rb3, rb4, rb5, rb6)

    recv_numbers, send_numbers, sent = {}, {}, []
    used = [0]

    def remote(key, src, dst, device):
        if key not in recv_numbers:
            recv_numbers[key] = len(recv_numbers)
            send_numbers[key] = used[0]
            used[0] += 1
        return pltpu.make_async_remote_copy(
            src_ref=src, dst_ref=dst, send_sem=send_sem.at[send_numbers[key]],
            recv_sem=recv_sem.at[recv_numbers[key]], device_id=device, device_id_type=MESH,
        )

    def launch(make):
        for c in make():
            c.start()
        sent.append(make)

    def flush():
        for make in sent:
            for c in make():
                c.wait_send()
        sent.clear()
        used[0] = 0

    def arrive(make):
        for c in make():
            c.wait_recv()

    weights = (
        wa.reshape(2, 2, 4, 2, BLOCK, D), wu.reshape(2, 2, 4, 2, BLOCK, D),
        wd.reshape(4, 2, 2, 2, BLOCK, D),
    )

    def held(kind, done, lane, width):
        every = slice(None)
        zz = every if done & LINE else d // 2
        xx = every if done & X else d % 2
        yy = every if done & Y else s // 2
        cc = every if done & CORE else s % 2
        at = (yy, cc, zz, xx) if kind < 2 else (zz, xx, yy, cc)
        return weights[kind].at[at + (every, pl.ds(lane, width))]

    def gather_copies(g, k):
        kind, lane, width, order = GATHERS[g]
        at = held(kind, sum(order[:k]), lane, width)
        return [
            remote(("g", g, k, f), at, at, place.away(f)) for f in subsets(order[k])[1:]
        ]

    def gather_stage(g, k):
        if k > 0:
            arrive(functools.partial(gather_copies, g, k - 1))
        if k < 3:
            launch(functools.partial(gather_copies, g, k))

    def vector_copies(k):
        return [
            remote(("v", k, f), vsend.at[k], vgot.at[k, n], place.away(f))
            for n, f in enumerate(subsets(VECTOR_ORDER[k])[1:])
        ]

    def vector_stage(k):
        if k > 0:
            arrive(functools.partial(vector_copies, k - 1))
            total = vsend[k - 1]
            for n in range(len(subsets(VECTOR_ORDER[k - 1])) - 1):
                total = total + vgot[k - 1, n]
            if k < 3:
                vsend[k] = total
            else:
                vec[...] = total.astype(F32)
        if k < 3:
            launch(functools.partial(vector_copies, k))

    def slab_copies():
        found = []
        for k in range(1, 4):
            j = (s + k) % 4
            found.append(remote(("s", k), slab.at[j], got.at[s], (d, j)))
        return found

    mine = pl.ds(pl.multiple_of(d * 8, 8), 8)

    def cls_copies(name, src, dst):
        found = []
        for k in range(1, owners):
            to = (d + k) % owners
            at = src.at[pl.ds(pl.multiple_of(to * 8, 8), 8)]
            found.append(remote((name, k), at, dst.at[mine], (to, s)))
        return found

    grads = (ga, gu, gd)

    def spans(g, k):
        order = REDUCES[g][3]
        rest = sum(order[k + 1 :])
        first = 0
        for i in range(k):
            first += (len(subsets(order[i])) - 1) * len(subsets(sum(order[i + 1 :])))
        return first, rest, len(subsets(rest))

    def reduce_copies(g, k):
        first, _, n = spans(g, k)
        found = []
        for i, f in enumerate(subsets(REDUCES[g][3][k])[1:]):
            at = pl.ds(first + i * n, n)
            found.append(
                remote(("r", g, k, f), sbufs[g].at[at], rbufs[g].at[at], place.away(f))
            )
        return found

    def reduce_stage(g, k):
        kind, lane, width, order = REDUCES[g]
        ref = grads[kind]
        if k > 0:
            arrive(functools.partial(reduce_copies, g, k - 1))

        def total(c):
            at = block_at(kind, place.away(c), lane, width)
            v = ref[at]
            if k > 0:
                first, rest, n = spans(g, k - 1)
                at_c = subsets(rest).index(c)
                for i in range(len(subsets(order[k - 1])) - 1):
                    v = v + rbufs[g][first + i * n + at_c].astype(F32)
            return at, v

        if k == 3:
            return total(0)[1]
        first, rest, n = spans(g, k)
        for i, f in enumerate(subsets(order[k])[1:]):
            for q, c in enumerate(subsets(rest)):
                sbufs[g][first + i * n + q] = total(f + c)[1].astype(BF)
        launch(functools.partial(reduce_copies, g, k))
        if k > 0:
            for c in subsets(rest):
                at, v = total(c)
                ref[at] = v

    def part_copies(slot):
        src, dst = (ps0, pg0) if slot == 0 else (ps1.at[slot - 1], pg1.at[slot - 1])
        found = []
        for k in range(1, 4):
            j = (s + k) % 4
            found.append(remote(("p", slot, k), src.at[j], dst.at[s], (d, j)))
        return found

    def count(full):
        g = full * full
        g = sum(g[:, i * 128 : (i + 1) * 128] for i in range(g.shape[1] // 128))
        square_buf[...] += sum(g[i * 8 : (i + 1) * 8] for i in range(g.shape[0] // 8))

    def to_all(buf, got_all, n):
        for to in peers:
            pltpu.make_async_remote_copy(
                src_ref=buf, dst_ref=got_all.at[flat],
                send_sem=all_sem.at[2 * n], recv_sem=all_sem.at[2 * n + 1],
                device_id=to, device_id_type=MESH,
            ).start()
        got_all[flat] = buf[...]

    def from_all(got_all, n):
        span = got_all.at[pl.ds(0, everyone - 1)]
        return pltpu.make_async_remote_copy(
            src_ref=span, dst_ref=span, send_sem=all_sem.at[2 * n],
            recv_sem=all_sem.at[2 * n + 1], device_id=peers[0], device_id_type=MESH,
        )

    def part_start(slot, full):
        count(full)
        src, dst = (ps0, pg0) if slot == 0 else (ps1.at[slot - 1], pg1.at[slot - 1])
        for j in range(4):
            src[j, 0:PART] = full[j * PART : (j + 1) * PART]
        launch(functools.partial(part_copies, slot))
        dst[s] = src[s]

    def part_end(slot):
        arrive(functools.partial(part_copies, slot))
        for j in range(4):
            if slot == 0:
                for t in range(3):
                    lin_u[pl.ds(3 * j + t, PART, stride=12), :] = pg0[
                        j, 0:PART, t * 128 : (t + 1) * 128
                    ]
            elif j < 3:
                lin_q[pl.ds(3 * j + slot - 1, PART, stride=9), :] = pg1[slot - 1, j, 0:PART]
            else:
                lin_o[pl.ds(slot - 1, PART, stride=3), :] = pg1[slot - 1, j, 0:PART]

    def up_end():
        full = jnp.concatenate([reduce_stage(0, 3), reduce_stage(1, 3)], axis=1)
        part_start(0, full)

    def down_end():
        full = jnp.concatenate([reduce_stage(2, 3), reduce_stage(3, 3)], axis=1)
        count(full)
        for t in range(3):
            lin_d[pl.ds(t, BLOCK, stride=3), :] = full[:, t * 128 : (t + 1) * 128]

    def sums_copies(k):
        return [
            remote(("w", k, f), gsend.at[k], ggot.at[k, n], place.away(f))
            for n, f in enumerate(subsets(SUMS_ORDER[k])[1:])
        ]

    def sums_stage(k):
        if k == 0:
            gsend[0] = gvec[...]
        else:
            arrive(functools.partial(sums_copies, k - 1))
            total = gsend[k - 1]
            for n in range(len(subsets(SUMS_ORDER[k - 1])) - 1):
                total = total + ggot[k - 1, n]
            if k == 3:
                return total
            gsend[k] = total
        launch(functools.partial(sums_copies, k))

    barrier = pltpu.get_barrier_semaphore()
    everyone = owners * 4
    flat = d * 4 + s
    peers = []
    for k in range(1, everyone):
        to = (flat + k) % everyone
        peers.append((to // 4, to % 4))
    for to in peers:
        pl.semaphore_signal(barrier, inc=1, device_id=to, device_id_type=MESH)

    shards = [
        pltpu.make_async_copy(src, dst, sem.at[2 * batches + i])
        for i, (src, dst) in enumerate(
            (
                (wq_hbm, wq), (wo_hbm, wo), (wu_hbm, wu_lin), (wd_hbm, wd_lin),
                (vector_hbm, vector), (cls_hbm, cls), (lengths_hbm, lengths), (routes_hbm, routes),
            )
        )
    ]
    for c in shards:
        c.start()
    copies = [
        pltpu.make_async_copy(x_hbm.at[0, b], x.at[b], sem.at[b]) for b in range(batches)
    ] + [
        pltpu.make_async_copy(og_hbm.at[0, b], dy.at[b], sem.at[batches + b])
        for b in range(batches)
    ]
    for c in copies:
        c.start()
    for c in shards:
        c.wait()

    for j in range(4):
        for t in range(3):
            c = 3 * j + t
            lanes = slice(t * 128, (t + 1) * 128)
            if j < 3:
                part = wq[pl.ds(c, PART, stride=9), :]
            else:
                part = wo[pl.ds(t, PART, stride=3), :]
            slab[j, 0, 0:PART, lanes] = part.astype(BF)
            slab[j, 1, 0:PART, lanes] = wu_lin[pl.ds(c, PART, stride=12), :].astype(BF)

    pl.semaphore_wait(barrier, len(peers))
    launch(slab_copies)
    vrows, vcols = vector_masks(place)
    vsend[0] = dg(jnp.where(vrows, vector[...], 0.0).astype(BF), vcols.astype(BF), NN).astype(BF)
    vector_stage(0)
    down_rows = pl.ds(pl.multiple_of(flat * BLOCK, 16), BLOCK)
    for t in range(3):
        wd[down_rows, t * 128 : (t + 1) * 128] = wd_lin[pl.ds(t, BLOCK, stride=3), :].astype(BF)
    got[s] = slab[s]
    gather_stage(4, 0)
    gather_stage(5, 0)

    arrive(slab_copies)
    for kind, ref in enumerate((wa, wu)):
        full = jnp.concatenate([got[j, kind].astype(F32)[0:PART] for j in range(4)], axis=0)
        ref[s, pl.ds(pl.multiple_of(d * BLOCK, 16), BLOCK), :] = full.astype(BF)
        if kind == 0:
            gather_stage(0, 0)
            gather_stage(1, 0)
    csend[...] = dg(slot_map((csend.shape[0], cls.shape[0]), 0, capacity), cls[...].astype(BF), NN)
    launch(functools.partial(cls_copies, "c", csend, ret))
    ret[mine, :] = csend[mine, :]

    def segment_of(t):
        return jnp.where(
            is_global,
            (t >= LG).astype(jnp.int32) + (t >= 2 * LG).astype(jnp.int32),
            lax.shift_right_logical(t * 1772, 16),
        )

    for i, (q0, k0, lo, hi) in enumerate(layout):
        keys = segment_of(iota((WIN, TILE), 0) + k0)
        queries = segment_of(iota((WIN, TILE), 1) + q0)
        mask = jnp.where(keys == queries, 0.0, MASK_VALUE).astype(F32)
        bias[i, :, :TILE] = mask
        bias[i, :, TILE:] = mask

    def v(row):
        return vec[row : row + 1, :]

    low_half = iota((TILE, TILE), 1) < HD

    def stack(t):
        z = jnp.zeros_like(t)
        return jnp.concatenate([jnp.where(low_half, t, z), jnp.where(low_half, z, t)], axis=0)

    def unstack(t):
        return jnp.where(low_half, t[:TILE], t[TILE:])

    def rows_at(b):
        return pl.ds(pl.multiple_of(b * rows, rows), rows)

    def hook(b, at, fn):
        @pl.when(b == at)
        def _():
            fn()

    gvec[...] = jnp.zeros_like(gvec)
    square_buf[...] = jnp.zeros_like(square_buf)
    for c in copies[:batches]:
        c.wait()

    def normed(b, c):
        y[b] = norm_stats(x[b])[0]
        return c

    lax.fori_loop(0, batches, normed, 0)
    vector_stage(1)
    gather_stage(0, 1)
    gather_stage(1, 1)

    def live_of(b):
        n = lengths[b, 0]
        for k in range(1, slots):
            n = n + lengths[b, k]
        return n

    def places(b, r):
        spot = jnp.full(r.shape, -1, jnp.int32)
        for k in range(slots):
            route = routes[b, k]
            padded = (route // capacity) * cap_pad + route % capacity
            padded = jnp.where(route >= 0, padded, -1)
            spot = jnp.where(r == padded, k * length, spot)
        return spot

    for c in copies[batches:]:
        c.wait()
    arrive(functools.partial(cls_copies, "c", csend, ret))

    def cotangent(b, c):
        rs = rows_at(b)
        nr = ret.shape[0]
        pick = (iota((rows, nr), 0) == places(b, iota((1, nr), 1))).astype(BF)
        live = iota((rows, D), 0) < live_of(b)
        g = dy[b] + dg(pick, ret[...].astype(BF), NN)
        g = jnp.where(live, g, 0.0)
        dy[b] = g
        g16 = g.astype(BF)
        dy16[rs, :] = g16
        gvec[7:8, :] += jnp.sum(g16.astype(F32), axis=0, keepdims=True)
        return c

    lax.fori_loop(0, batches, cotangent, 0)
    vector_stage(2)
    gather_stage(0, 2)
    gather_stage(1, 2)
    gather_stage(2, 0)
    gather_stage(3, 0)
    o[...] = jnp.zeros_like(o)
    gu[...] = jnp.zeros_like(gu)
    gdt[...] = jnp.zeros_like(gdt)
    ga[:, 3 * D :] = jnp.zeros((D, D), F32)
    heads[...] = jnp.zeros_like(heads)
    vector_stage(3)
    gather_stage(0, 3)
    gather_stage(1, 3)

    def attend(b, c):
        rs = rows_at(b)
        h = (y[b] * v(0) + v(1)).astype(BF)
        h1[rs, :] = h
        h1t[:, rs] = h.T
        p[rs, 0:D] = (dg(h, wa[0], NN) + v(2)).astype(BF)
        p[rs, D : 2 * D] = dg(h, wa[1], NN).astype(BF)
        p[rs, 2 * D : 3 * D] = (dg(h, wa[2], NN) + v(3)).astype(BF)
        for pair in range(PAIRS):
            c0 = pair * TILE
            for i, (q0, k0, lo, hi) in enumerate(layout):
                qr = pl.ds(pl.multiple_of(b * rows + q0, 16), TILE)
                kr = pl.ds(pl.multiple_of(b * rows + k0, 16), WIN)
                q = stack(p[qr, pl.ds(c0, TILE)] * BF(HD**-0.5))
                k = p[kr, pl.ds(D + c0, TILE)]
                val = p[kr, pl.ds(2 * D + c0, TILE)]
                sc = dg(k, q, NT) + bias[i]
                e = jnp.exp(sc - jnp.max(sc, axis=0, keepdims=True))
                a = (e * (1.0 / jnp.sum(e, axis=0, keepdims=True))).astype(BF)
                att[b, pair, i] = a
                r = unstack(dg(a, val, TN)).astype(BF)
                own = iota((TILE, TILE), 0) + q0
                own = (own >= lo) & (own < hi)
                old = o[qr, pl.ds(c0, TILE)]
                o[qr, pl.ds(c0, TILE)] = jnp.where(own, r, old)
        hook(b, 0, lambda: [gather_stage(g, 1) for g in range(2, 6)])
        return c

    lax.fori_loop(0, batches, attend, 0)

    def middle(b, c):
        mid = x[b] + (dg(o[rows_at(b), :], wa[3], NN) + v(4))
        y[b] = mid
        h2[rows_at(b), :] = (norm_stats(mid)[0] * v(5) + v(6)).astype(BF)
        return c

    lax.fori_loop(0, batches, middle, 0)
    for g in range(2, 6):
        gather_stage(g, 2)
    for j in range(4):
        bup[0:1, j * D : (j + 1) * D] = v(8 + j)
    gbup[...] = jnp.zeros_like(gbup)
    for g in range(2, 6):
        gather_stage(g, 3)

    third = FF // 3

    def up(first, last):
        pieces = []
        for i in range(4):
            lo, hi = max(first, i * D), min(last, (i + 1) * D)
            if lo < hi:
                pieces.append(wu[i, :, lo - i * D : hi - i * D])
        return jnp.concatenate(pieces, axis=1) if len(pieces) > 1 else pieces[0]

    def inner(b, c):
        rs = rows_at(b)
        for j in range(3):
            cs = slice(j * third, (j + 1) * third)
            u = dg(h2[rs, :], up(cs.start, cs.stop), NN) + bup[0:1, cs]
            g, slope = gelu_parts(u)
            gb[:, cs] = g.astype(BF)
            du = (dg(dy16[rs, :], wd[cs, :], NT) * slope).astype(BF)
            dub[:, cs] = du
            gbup[0:1, cs] += jnp.sum(du.astype(F32), axis=0, keepdims=True)
        d2 = dg(dub[...], up(0, FF), NT)
        for j in range(3):
            cs = slice(j * third, (j + 1) * third)
            gdt[:, cs] += dg(dy16[rs, :], gb[:, cs], TN)
            gu[:, cs] += dg(h2[rs, :], dub[:, cs], TN)
        live = iota((rows, D), 0) < live_of(b)
        mid = y[b]
        out = jnp.where(live, mid + (dg(gb[...], wd[...], NN) + v(7)), 0.0)
        y[b] = out
        nr = heads.shape[0]
        pick = (places(b, iota((nr, 1), 0)) == iota((nr, rows), 1)).astype(BF)
        heads[...] += dg(pick, out.astype(BF), NN)
        xhat, r = norm_stats(mid)
        gvec[5:6, :] += jnp.sum(d2 * xhat, axis=0, keepdims=True)
        gvec[6:7, :] += jnp.sum(d2, axis=0, keepdims=True)
        dm = dy[b] + norm_back(d2, v(5), xhat, r)
        dy[b] = dm
        d16 = dm.astype(BF)
        gvec[4:5, :] += jnp.sum(d16.astype(F32), axis=0, keepdims=True)
        ga[:, 3 * D :] += dg(o[rs, :], d16, TN)
        h2[rs, :] = dg(d16, wa[3], NT).astype(BF)
        return c

    flush()
    lax.fori_loop(0, batches, inner, 0)
    for j in range(4):
        gvec[8 + j : 9 + j, :] = gbup[0:1, j * D : (j + 1) * D]
    for g in range(2):
        reduce_stage(g, 0)
    gd[...] = gdt[...].T
    for g in range(2, 4):
        reduce_stage(g, 0)
    launch(functools.partial(cls_copies, "h", heads, cgot))
    cgot[mine, :] = heads[mine, :]

    hooks = {
        (0, 3): lambda: [reduce_stage(g, 1) for g in range(4)],
        (1, 1): lambda: reduce_stage(4, 1),
        (2, 1): lambda: reduce_stage(4, 2),
        (2, 2): lambda: [reduce_stage(g, 2) for g in range(4)],
        (2, 3): lambda: reduce_stage(5, 1),
    }
    for pair in range(PAIRS):
        c0 = pair * TILE

        def attend_back(b, c, pair=pair, c0=c0):
            rs = rows_at(b)
            y_k, y_v = hat.at[:, 0:TILE], hat.at[:, TILE : 2 * TILE]
            dqs[...] = jnp.zeros_like(dqs)
            hat[...] = jnp.zeros((rows, 2 * TILE), F32)
            where = []
            for i, (q0, k0, lo, hi) in enumerate(layout):
                qr = pl.ds(pl.multiple_of(b * rows + q0, 16), TILE)
                kr = pl.ds(pl.multiple_of(b * rows + k0, 16), WIN)
                wr = pl.ds(pl.multiple_of(k0, 16), WIN)
                own = iota((TILE, TILE), 0) + q0
                own = (own >= lo) & (own < hi)
                where.append((i, qr, kr, wr, own))

            def grad_stack(qr, own):
                do = h2[qr, pl.ds(c0, TILE)]
                return stack(jnp.where(own, do, jnp.zeros_like(do)))

            das = [
                dg(p[kr, pl.ds(2 * D + c0, TILE)], grad_stack(qr, own), NT)
                for i, qr, kr, wr, own in where
            ]
            dss = []
            for (i, qr, kr, wr, own), da in zip(where, das):
                af = att[b, pair, i].astype(F32)
                t = af * da
                dss.append((t - af * jnp.sum(t, axis=0, keepdims=True)).astype(BF))
            for (i, qr, kr, wr, own), ds in zip(where, dss):
                q = stack(p[qr, pl.ds(c0, TILE)] * BF(HD**-0.5))
                y_k[wr, :] += dg(ds, q, NN)
                y_v[wr, :] += dg(att[b, pair, i], grad_stack(qr, own), NN)
                dq = unstack(dg(ds, p[kr, pl.ds(D + c0, TILE)], TN)) * HD**-0.5
                at = pl.ds(pl.multiple_of(layout[i][0], 16), TILE)
                dqs[at, :] = jnp.where(own, dq.astype(BF), dqs[at, :])
            p[rs, c0 : c0 + TILE] = dqs[...]
            p[rs, D + c0 : D + c0 + TILE] = y_k[...].astype(BF)
            p[rs, 2 * D + c0 : 2 * D + c0 + TILE] = y_v[...].astype(BF)
            for (at_pair, at_b), fn in hooks.items():
                if at_pair == pair:
                    hook(b, at_b, fn)
            return c

        lax.fori_loop(0, batches, attend_back, 0)
        dp = jnp.concatenate([p[:, i * D + c0 : i * D + c0 + TILE] for i in range(3)], axis=1)
        g = dg(h1t[...], dp, NN)
        sums = jnp.sum(dp.astype(F32), axis=0, keepdims=True)
        gvec[2:3, c0 : c0 + TILE] = sums[:, 0:TILE]
        gvec[3:4, c0 : c0 + TILE] = sums[:, 2 * TILE :]
        for i in range(3):
            ga[:, i * D + c0 : i * D + c0 + TILE] = g[:, i * TILE : (i + 1) * TILE]
        reduce_stage(4 + pair, 0)

    sums_stage(0)

    def last(b, c):
        xhat, r = norm_stats(x[b])
        whole = jnp.concatenate([wa[i] for i in range(3)], axis=1)
        d1 = dg(p[rows_at(b), :], whole, NT)
        gvec[0:1, :] += jnp.sum(d1 * xhat, axis=0, keepdims=True)
        gvec[1:2, :] += jnp.sum(d1, axis=0, keepdims=True)
        dy[b] += norm_back(d1, v(0), xhat, r)
        hook(b, 0, lambda: (reduce_stage(6, 1), sums_stage(1)))
        hook(b, 1, lambda: (part_start(1, reduce_stage(4, 3)), reduce_stage(5, 2)))
        hook(b, 2, lambda: (up_end(), down_end()))
        return c

    lax.fori_loop(0, batches, last, 0)
    for t in range(3):
        late_buf[t : t + 1, :] = gvec[0:1, t * 128 : (t + 1) * 128]
        late_buf[3 + t : 4 + t, :] = gvec[1:2, t * 128 : (t + 1) * 128]
    to_all(late_buf, late_got, 0)
    reduce_stage(6, 2)
    sums_stage(2)
    part_start(2, reduce_stage(5, 3))
    part_end(1)
    part_end(0)
    arrive(functools.partial(cls_copies, "h", heads, cgot))
    pick = slot_map((cls_out.shape[0], cgot.shape[0]), 1, capacity)
    cls_out[...] = dg(pick, cgot[...].astype(BF), NN)
    part_end(2)
    sums = sums_stage(3)
    from_all(late_got, 0).wait_recv()
    late = late_got[0]
    for k in range(1, everyone):
        late = late + late_got[k]
    ends = [
        jnp.concatenate([late[3 * i + t : 3 * i + t + 1, :] for t in range(3)], axis=1)
        for i in range(2)
    ]
    sums = jnp.concatenate([ends[0], ends[1], sums[2:, :]], axis=0)
    own_sums = lax.dot_general(
        sums, vcols.astype(F32), NT, precision=lax.Precision.HIGHEST, preferred_element_type=F32
    )
    own_sums = jnp.sum(jnp.where(vrows, own_sums, 0.0), axis=0, keepdims=True)
    span = own_sums.shape[1]
    lin[440:441, :] = own_sums[:, 0:128]
    lin[441:442, 0 : span - 128] = own_sums[:, 128:span]
    part_start(3, reduce_stage(6, 3))

    squares = jnp.sum(square_buf[...], axis=0, keepdims=True)
    squares = jnp.sum(squares, axis=1, keepdims=True)
    squares = squares + jnp.sum(own_sums * own_sums, axis=1, keepdims=True)
    square_buf[...] = jnp.broadcast_to(squares, (8, 128))

    to_all(square_buf, square_got, 1)
    part_end(3)
    from_all(square_got, 1).wait_recv()
    total = square_got[0]
    for k in range(1, everyone):
        total = total + square_got[k]
    lin[442:443, :] = jnp.sqrt(total)[0:1]
    for i, got_all in enumerate((late_got, square_got)):
        from_all(got_all, i).wait_send()
    flush()


def run_step(lengths, routes, x, og, masters, cls, owners, capacity):
    qkv, out, up, down, vector = masters
    lin = [w.reshape(-1, 128) for w in (qkv, out, up, down)] + [vector.reshape(1, -1), cls]
    batches, rows = x.shape[1], x.shape[2]
    total = batches * rows
    slots = owners * 8
    vm = pl.BlockSpec(memory_space=VM)
    anyspace = pl.BlockSpec(memory_space=pl.ANY)
    act = VM((total, D), BF)
    scratch = [VM(w.shape, F32) for w in lin]
    scratch += [pltpu.SMEM(lengths.shape, jnp.int32), pltpu.SMEM(routes.shape, jnp.int32)]
    scratch += [
        VM((batches, rows, D), F32), VM((rows, 2 * TILE), F32),
        act, VM((D, total), BF), VM((total, 3 * D), BF),
        VM((batches, PAIRS, 4, WIN, 2 * TILE), BF),
        act, act, act, VM((rows, FF), BF), VM((rows, FF), BF), VM((D, FF), F32),
        VM((8, FF), F32), VM((8, FF), F32), VM((rows, TILE), BF), VM((4, WIN, 2 * TILE), F32),
        VM((4, D, D), BF), VM((4, D, D), BF), VM((FF, D), BF),
        VM((D, 4 * D), F32), VM((D, FF), F32), VM((FF, D), F32),
        VM((16, D), F32), VM((16, D), F32),
        VM((slots, D), F32), VM((slots, D), F32), VM((slots, D), F32), VM((slots, D), F32),
        VM((4, 2, 16, D), BF), VM((4, 2, 16, D), BF),
        VM((3, 16, D), BF), VM((3, 3, 16, D), BF), VM((3, 16, D), F32), VM((3, 3, 16, D), F32),
    ]
    buffers = [VM((31, BLOCK, r[2]), BF) for r in REDUCES]
    scratch += buffers + buffers
    scratch += [
        VM((4, 16, D), F32), VM((3, 4, 16, 128), F32),
        VM((4, 16, D), F32), VM((3, 4, 16, 128), F32),
        VM((8, 128), F32), VM((owners * 4, 8, 128), F32),
        VM((8, 128), F32), VM((owners * 4, 8, 128), F32),
        pltpu.SemaphoreType.DMA((2 * batches + 10,)),
        pltpu.SemaphoreType.DMA((84,)), pltpu.SemaphoreType.DMA((140,)),
        pltpu.SemaphoreType.DMA((4,)),
    ]
    return pl.pallas_call(
        functools.partial(step_kernel, owners=owners, capacity=capacity),
        out_shape=(
            VM(x.shape[1:], F32), VM(x.shape[1:], F32), VM((448, 128), F32), VM(cls.shape, F32),
        ),
        in_specs=[anyspace] * 10,
        out_specs=(vm,) * 4,
        scratch_shapes=scratch,
        compiler_params=pltpu.CompilerParams(
            collective_id=1, has_side_effects=True, vmem_limit_bytes=56 * 2**20
        ),
        name="step",
    )(lengths, routes, x, og, *lin)


def adam_terms(master, first, second, gradient, factor, rate, decay):
    clipped = gradient * factor
    mean = BETA_ONE * first + (1.0 - BETA_ONE) * clipped
    square = BETA_TWO * second + (1.0 - BETA_TWO) * clipped * clipped
    mean_hat = mean / (1.0 - BETA_ONE**STEP_NUM)
    square_hat = square / (1.0 - BETA_TWO**STEP_NUM)
    step = mean_hat / (jnp.sqrt(square_hat) + ADAM_EPSILON)
    return master - rate * (step + decay * master), mean, square


def update_kernel(*refs):
    big_in, cls_in, grad, state_in = refs[0:2], refs[2], refs[3], refs[4:19]
    big_out, cls_out, norm_out, state_out = refs[19:21], refs[21], refs[22], refs[23:38]
    norm, state, results, sem = refs[38], refs[39:54], refs[54:69], refs[69]
    batches = big_in[0].shape[0]
    n = [0]

    def go(src, dst):
        c = pltpu.make_async_copy(src, dst, sem.at[n[0]])
        n[0] += 1
        c.start()
        return c

    ins = [go(a, b) for a, b in zip(state_in, state)]
    outs = [
        go(src.at[b], dst.at[0, b]) for src, dst in zip(big_in, big_out) for b in range(batches)
    ]
    outs.append(go(cls_in, cls_out))
    for c in ins:
        c.wait()
    norm[...] = grad[442:443, 0:1]
    outs.append(go(norm, norm_out))
    factor = jnp.minimum(1.0, CLIP_LIMIT / grad[442:443, 0:1])
    span = state[4].shape[1]
    grads = [
        grad[0:108], grad[112:148], grad[152:296], grad[296:440],
        jnp.concatenate([grad[440:441, :], grad[441:442, 0 : span - 128]], axis=1),
    ]
    for i in range(5):
        rate, decay = (RATE_VECTOR, 0.0) if i == 4 else (RATE_MATRIX, WEIGHT_DECAY)
        new = adam_terms(
            state[i][...], state[5 + i][...], state[10 + i][...], grads[i], factor, rate, decay
        )
        for k in range(3):
            results[5 * k + i][...] = new[k]
            outs.append(go(results[5 * k + i], state_out[5 * k + i]))
    for c in outs:
        c.wait()


def run_update(block_out, input_grad, grads, cls_grouped, state):
    flat = [w.reshape(1, -1) if i % 5 == 4 else w.reshape(-1, 128) for i, w in enumerate(state)]
    vm = pl.BlockSpec(memory_space=VM)
    anyspace = pl.BlockSpec(memory_space=pl.ANY)
    large = (1,) + block_out.shape
    shapes = [large, large, cls_grouped.shape, (1, 1)] + [w.shape for w in flat]
    buffers = [VM(w.shape, F32) for w in flat]
    return pl.pallas_call(
        update_kernel,
        out_shape=tuple(jax.ShapeDtypeStruct(z, F32) for z in shapes),
        in_specs=[vm] * 4 + [anyspace] * 15,
        out_specs=(anyspace,) * 19,
        scratch_shapes=[VM((1, 1), F32)] + buffers + buffers + [pltpu.SemaphoreType.DMA((64,))],
        compiler_params=pltpu.CompilerParams(vmem_limit_bytes=16 * 2**20),
        name="update",
    )(block_out, input_grad, cls_grouped, grads, *flat)


def local_fast(tokens, out_grad, cls_grad, crop_lengths, cls_route, *state):
    owners = lax.axis_size("dp")
    capacity = cls_grad.shape[0] // owners
    block_out, input_grad, grads, cls_grouped = run_step(
        crop_lengths[0], cls_route[0], tokens, out_grad, state[:5], cls_grad, owners, capacity
    )
    new = run_update(block_out, input_grad, grads, cls_grouped, state)
    rest = tuple(w.reshape(-1) for w in new[4:])
    return (new[0], new[2], new[1], new[3].reshape(())) + rest


def solution(mesh):
    spread = ("dp", "shard")
    in_specs = (
        P(spread, None, None, None), P(spread, None, None, None), P(spread, None),
        P(spread, None, None), P(spread, None, None),
    ) + (P(spread),) * 15
    out_specs = (
        P(spread, None, None, None), P(spread, None), P(spread, None, None, None), P(),
    ) + (P(spread),) * 15
    fast = mesh.shape["shard"] == 4 and mesh.shape["dp"] == 8
    body = local_fast if fast else local
    return jax.shard_map(body, mesh=mesh, in_specs=in_specs, out_specs=out_specs, check_vma=False)
```
